32 devices in a mesh: row: 4 (over y, x), col: 4 (over z), depth: 2 (over core).
Axes of the slice: x: 2, y: 2, z: 4, core: 2. Of those that a mesh axis runs over, the one named last changes fastest.
Arguments:
- a_blocks: bfloat16 [32, 32, 2, 128, 128], P(('row', 'col', 'depth')), may hold values from -1.25 to 1.25
- a_columns: int32 [32, 32, 2], P(('row', 'col', 'depth')), may hold values from 0 to 319, as said below
- a_live: int32 [32, 32, 2], P(('row', 'col', 'depth')), may hold values from 0 to 1
- atom_rows: int32 [32], P(('row', 'col', 'depth')), may hold values from 0 to 31, as said below
- b_blocks: bfloat16 [320, 4, 6, 128, 128], P(('row', 'depth'), 'col'), may hold values from -1.25 to 1.25
- b_columns: int32 [320, 4, 6], P(('row', 'depth'), 'col'), may hold values from 0 to 319, as said below
- b_live: int32 [320, 4, 6], P(('row', 'depth'), 'col'), may hold values from 0 to 1, as said below
- c_columns: int32 [32, 4, 8], P('row', 'col'), may hold values from 0 to 319, as said below
- c_live: int32 [32, 4, 8], P('row', 'col'), may hold values from 0 to 1
Outputs:
- product: bfloat16 [32, 4, 8, 128, 128], P('row', 'col', 'depth')
The draws below stay inside these ranges and needn't reach their ends.
Inputs may be any that keep to these rules, and one draw needn't show every extreme that they name: `a_columns`: columns of one block row and group g are distinct and lie in g * 10 to (g + 1) * 10 - 1, also in empty slots. `atom_rows`: A permutation that maps every aligned run of 8 atom-order rows onto the same run of block rows. `b_columns`: columns of one block row and panel c are distinct and lie in c * 80 to (c + 1) * 80 - 1, also in empty slots. `b_live`: live slots of block row k hold columns within 16 of k, counted round. `c_columns`: columns of one block row and panel c are distinct and lie in c * 80 to (c + 1) * 80 - 1.
All inputs are finite; a program needn't handle non-finite values.
Results may differ from the reference program's by a relative error of at most 0.0043.
Values may be sent and summed in bfloat16 or wider, within the bound.
A program may use at most 320 MiB of HBM per device.

```python
import jax
import jax.numpy as jnp
from jax import lax

BS = 128
NB = 320
GW = 10
KR = 2
KBR = 6
KC = 8
R = 8
MB = 32
CW = 80
N_ROW = 4
N_COL = 4
N_DEPTH = 2


def distinct_pick(key, lead_shape, width, take):
    scores = jax.random.randint(key, lead_shape + (width,), 0, 1 << 20, dtype=jnp.int32)
    scores = scores * width + jnp.arange(width, dtype=jnp.int32)
    ordering = jnp.argsort(scores, axis=-1, stable=True)
    return ordering[..., :take].astype(jnp.int32)


def cycle_distance(first, second):
    gap = (first - second) % NB
    return jnp.minimum(gap, NB - gap)


def atom_order(key):
    run_count = MB // R
    ordering = distinct_pick(jax.random.fold_in(key, 13), (run_count,), R, R)
    return (ordering + (jnp.arange(run_count, dtype=jnp.int32) * R)[:, None]).reshape(MB)


def a_pattern(key):
    groups = NB // GW
    chosen = distinct_pick(jax.random.fold_in(key, 11), (MB, groups), GW, KR)
    columns = chosen + (jnp.arange(groups, dtype=jnp.int32) * GW)[None, :, None]
    block_row = atom_order(key)
    center = block_row * NB // MB
    group_middle = jnp.arange(groups, dtype=jnp.int32) * GW + GW // 2
    near = cycle_distance(group_middle[None, :], center[:, None]) <= 7 * GW
    favored = (center // GW)[:, None] == jnp.arange(groups, dtype=jnp.int32)[None, :]
    counts = jax.random.randint(jax.random.fold_in(key, 12), (MB, groups), 1, KR + 1, dtype=jnp.int32)
    far_counts = jax.random.randint(jax.random.fold_in(key, 18), (MB, groups), 0, KR + 1, dtype=jnp.int32)
    counts = jnp.where(favored, KR, jnp.where(near, counts, far_counts))
    live = (jnp.arange(KR, dtype=jnp.int32) < counts[..., None]).astype(jnp.int32)
    return (columns, live)


def b_pattern(key):
    panels = NB // CW
    noise = jax.random.randint(jax.random.fold_in(key, 14), (NB, panels, CW), 0, 1 << 16, dtype=jnp.int32)
    cells = jnp.arange(panels, dtype=jnp.int32)[:, None] * CW + jnp.arange(CW, dtype=jnp.int32)[None, :]
    near = cycle_distance(cells[None, :, :], jnp.arange(NB, dtype=jnp.int32)[:, None, None]) <= 16
    scores = (near.astype(jnp.int32) * (1 << 16) + noise) * CW + jnp.arange(CW, dtype=jnp.int32)
    order = jnp.argsort(-scores, axis=-1, stable=True)[..., :KBR].astype(jnp.int32)
    columns = order + (jnp.arange(panels, dtype=jnp.int32) * CW)[None, :, None]
    kept = jax.random.randint(jax.random.fold_in(key, 15), (NB, panels, KBR), 0, 4, dtype=jnp.int32)
    live = jnp.take_along_axis(near.astype(jnp.int32), order, axis=-1) * (kept > 0).astype(jnp.int32)
    return (columns, live)


def c_pattern(key):
    panels = NB // CW
    a_cols, a_flags = a_pattern(key)
    b_cols, b_flags = b_pattern(key)
    block_row = atom_order(key)
    positions = jnp.arange(NB, dtype=jnp.int32)
    a_hot = jnp.sum(((a_cols[..., None] == positions) & (a_flags[..., None] > 0)).astype(jnp.int32), axis=(1, 2))
    b_hot = jnp.sum(((b_cols[..., None] == positions) & (b_flags[..., None] > 0)).astype(jnp.int32), axis=(1, 2))
    reach_atom = jnp.dot(a_hot, b_hot, preferred_element_type=jnp.int32)
    inverse = jnp.zeros((MB,), jnp.int32).at[block_row].set(jnp.arange(MB, dtype=jnp.int32))
    reach = reach_atom[inverse].reshape(MB, panels, CW)
    noise = jax.random.randint(jax.random.fold_in(key, 16), (MB, panels, CW), 0, 1 << 12, dtype=jnp.int32)
    scores = (jnp.minimum(reach, 255) * (1 << 12) + noise) * CW + jnp.arange(CW, dtype=jnp.int32)
    order = jnp.argsort(-scores, axis=-1, stable=True)[..., :KC].astype(jnp.int32)
    columns = order + (jnp.arange(panels, dtype=jnp.int32) * CW)[None, :, None]
    reached = jnp.take_along_axis(reach, order, axis=-1)
    dropped = jax.random.randint(jax.random.fold_in(key, 17), (MB, panels, KC), 0, 8, dtype=jnp.int32)
    live = ((reached > 0) & (dropped > 0)).astype(jnp.int32)
    return (columns, live)


def draw_a_columns(key, part):
    return a_pattern(key)[0]


def draw_a_live(key, part):
    return a_pattern(key)[1]


def draw_atom_rows(key, part):
    return atom_order(key)


def draw_b_columns(key, part):
    return b_pattern(key)[0]


def draw_b_live(key, part):
    return b_pattern(key)[1]


def draw_c_columns(key, part):
    return c_pattern(key)[0]


def draw_c_live(key, part):
    return c_pattern(key)[1]


def block_scale(own_key, dims, split, smallest, largest):
    def one(axis_at, parts):
        draws = jax.random.uniform(jax.random.fold_in(jax.random.fold_in(own_key, 6), axis_at), (parts,), jnp.float32, smallest / len(split), largest / len(split))
        return jnp.repeat(jnp.exp(draws), dims[axis_at] // parts).reshape((-1,) + (1,) * (len(dims) - axis_at - 1))

    level = one(*split[0])
    for cut in split[1:]:
        level = level * one(*cut)
    return level


def normal_values(stream_key, shape, scale, limit, cuts=(), kind=jnp.bfloat16):
    entries = jax.random.normal(stream_key, shape, jnp.float32) * scale
    if len(cuts) > 0:
        entries = block_scale(stream_key, shape, cuts, -0.22, 0.18) * entries
    return jnp.clip(entries, min=-limit, max=limit).astype(kind)


def setup_inputs(seed: int = 0) -> dict:
    key_list = jax.random.split(jax.random.key(seed), 10)
    a_blocks = normal_values(key_list[0], (MB, NB // GW, KR, BS, BS), (0.7 * BS ** -0.25), 1.25, ((0, 32),))
    a_columns = draw_a_columns(jax.random.fold_in(key_list[9], 71), 0)
    a_live = draw_a_live(jax.random.fold_in(key_list[9], 71), 0)
    atom_rows = draw_atom_rows(jax.random.fold_in(key_list[9], 71), 0)
    b_blocks = normal_values(key_list[4], (NB, NB // CW, KBR, BS, BS), (0.7 * BS ** -0.25), 1.25, ((0, 8), (1, 4)))
    b_columns = draw_b_columns(jax.random.fold_in(key_list[9], 71), 0)
    b_live = draw_b_live(jax.random.fold_in(key_list[9], 71), 0)
    c_columns = draw_c_columns(jax.random.fold_in(key_list[9], 71), 0)
    c_live = draw_c_live(jax.random.fold_in(key_list[9], 71), 0)
    return {"a_blocks": a_blocks, "a_columns": a_columns, "a_live": a_live, "atom_rows": atom_rows, "b_blocks": b_blocks, "b_columns": b_columns, "b_live": b_live, "c_columns": c_columns, "c_live": c_live}


def reference(a_blocks, a_columns, a_live, atom_rows, b_blocks, b_columns, b_live, c_columns, c_live):
    stripe = NB // (N_ROW * N_DEPTH)
    panel_ids = jnp.arange(N_COL, dtype=jnp.int32)
    layer_ids = jnp.arange(N_DEPTH, dtype=jnp.int32)
    inverse = jnp.zeros((MB,), jnp.int32).at[atom_rows].set(jnp.arange(MB, dtype=jnp.int32))

    def one_row(target_row):
        source = inverse[target_row]
        block_tiles = a_blocks[source].reshape(-1, BS, BS)
        columns = a_columns[source].reshape(-1)
        live_flags = a_live[source].reshape(-1)
        found_columns = jnp.transpose(b_columns[columns], (1, 0, 2))
        found_live = jnp.transpose(b_live[columns], (1, 0, 2))
        wanted = c_columns[target_row]
        matched_pairs = (found_columns[:, None, :, :] == wanted[:, :, None, None]) & (found_live[:, None, :, :] > 0) & (live_flags[None, None, :, None] > 0)
        present = jnp.any(matched_pairs, axis=-1)
        slot_index = jnp.sum(jnp.where(matched_pairs, jnp.arange(KBR, dtype=jnp.int32), 0), axis=-1).astype(jnp.int32)
        selected_entries = b_blocks[columns[None, None, :], panel_ids[:, None, None], slot_index]
        selected_entries = jnp.where(present[..., None, None], selected_entries, jnp.zeros((), selected_entries.dtype))
        block_products = jnp.einsum('kqy,pckyt->pckqt', block_tiles.astype(jnp.float32), selected_entries.astype(jnp.float32))
        layer_of = (columns // stripe) % N_DEPTH
        selector = (layer_of[:, None] == layer_ids[None, :]).astype(jnp.float32)
        partial_sums = jnp.einsum('xuvae,vd->dxuae', block_products, selector)
        rounded = lax.optimization_barrier(partial_sums.astype(jnp.bfloat16))
        summed = jnp.sum(rounded.astype(jnp.float32), axis=0)
        summed = jnp.where(c_live[target_row][..., None, None] > 0, summed, jnp.float32(0.0))
        return summed.astype(jnp.bfloat16)

    return lax.map(one_row, jnp.arange(MB, dtype=jnp.int32))
```

```python
import functools

import jax
import jax.numpy as jnp
from jax import lax
from jax.experimental import pallas as pl
from jax.experimental.pallas import tpu as pltpu
from jax.sharding import PartitionSpec as P

GW = 10
REACH = 16
MESH = pl.DeviceIdType.MESH


def stripe_kinds(total, stripe, panel):
    kinds = {}
    for rel in range(total // stripe):
        groups = []
        for g in range(stripe // GW):
            first = rel * stripe + g * GW
            if any((k + REACH) % total < panel + 2 * REACH for k in range(first, first + GW)):
                groups.append(g)
        if groups:
            kinds[rel] = (groups[0], groups[-1] + 1)
    return kinds


def flip(index, step, count):
    return lax.rem(index // 2 + step // 2, count // 2) * 2 + lax.rem(index + step, 2)


def kernel(
    n_row, n_col, n_depth, kinds, slots,
    pack_ref, keys_ref, keep_ref, a_ref, b_ref, out_ref,
    lbuf, picks, pick_s, abuf, bbuf, cbuf, mbuf, pbuf,
    l_send, l_recv, s_sem, b_sem, a_send, a_recv, m_send, m_recv, m_free, c_send, c_recv,
):
    row, col, depth = (lax.axis_index(name) for name in ("row", "col", "depth"))
    stripes = n_row * n_depth
    per_panel = stripes // n_col
    run = n_col * n_depth
    rows = n_row * run
    me = (row * n_col + col) * n_depth + depth
    my_stripe = row * n_depth + depth
    my_rel = lax.rem(my_stripe - per_panel * col + stripes, stripes)
    rels = sorted(kinds)
    blocks = b_ref.shape[0]
    share = pbuf.shape[2]
    targets = share * n_depth
    width = a_ref.shape[0] // stripes
    groups = width // slots
    active = functools.reduce(jnp.logical_or, [my_rel == rel for rel in rels])
    paired = [rel for rel in rels if rel ^ 1 in kinds and n_depth == 2]
    lone = [rel for rel in rels if rel not in paired]
    senders = sorted({rel // 2 * 2 if rel in paired else rel for rel in rels})

    def sender(rel):
        return senders.index(rel // 2 * 2 if rel in paired else rel)

    def a_part(ref, rel):
        low, high = kinds[rel]
        return ref.at[pl.ds(low * slots, (high - low) * slots)]

    def list_copy(offset):
        dest = lax.rem(me + offset, rows)
        dest_row, dest_col, dest_depth = dest // run, dest // n_depth % n_col, dest % n_depth
        return pltpu.make_async_remote_copy(
            src_ref=pack_ref.at[dest_row * n_depth + dest_depth],
            dst_ref=lbuf.at[me],
            send_sem=l_send,
            recv_sem=l_recv,
            device_id=(dest_row, dest_col, dest_depth),
            device_id_type=MESH,
        )

    pltpu.make_async_copy(pack_ref.at[my_stripe], lbuf.at[me], l_recv).start()

    def send_list(offset, carry):
        list_copy(offset).start()
        return carry

    lax.fori_loop(1, rows, send_list, 0)

    b_copy = pltpu.make_async_copy(b_ref, bbuf.at[pl.ds(0, blocks)], b_sem)

    @pl.when(active)
    def _():
        b_copy.start()

    sends = []
    for t in reversed(range(n_col)):
        c = flip(row, t, n_col)
        for rel in rels:
            s = lax.rem(per_panel * c + rel, stripes)
            low, high = kinds[rel]
            src = a_ref.at[pl.ds(s * width + low * slots, (high - low) * slots)]
            mine = (my_stripe == s) & (col == c)
            remote = pltpu.make_async_remote_copy(
                src_ref=src,
                dst_ref=a_part(abuf.at[me], rel),
                send_sem=a_send.at[len(sends)],
                recv_sem=a_recv.at[me],
                device_id=(s // n_depth, c, s % n_depth),
                device_id_type=MESH,
            )
            local = pltpu.make_async_copy(src, a_part(abuf.at[me], rel), a_recv.at[me])
            sends.append((mine, remote))

            @pl.when(mine)
            def _(local=local):
                local.start()

            @pl.when(jnp.logical_not(mine))
            def _(remote=remote):
                remote.start()

    for rel in rels:
        low, high = kinds[rel]
        gaps = [g for g in range(groups) if not low <= g < high]
        if gaps:

            @pl.when(my_rel == rel)
            def _(gaps=gaps):
                def clear(p, carry):
                    for g in gaps:
                        for v in range(g * slots, (g + 1) * slots):
                            abuf[p, v] = jnp.zeros(abuf.shape[2:], abuf.dtype)
                    return carry

                lax.fori_loop(0, rows, clear, 0)

    pltpu.make_async_copy(lbuf, lbuf, l_recv).wait()
    lanes = lbuf.shape[2]

    def match(p, carry):
        column_row = lbuf[p, 0:1, :]
        place = lbuf[p, 1:2, :]
        table = lbuf[(p // run * n_col + col) * n_depth, 8:, :]
        at = lax.broadcasted_iota(jnp.int32, (run, lanes), 0)
        wanted = jnp.sum(jnp.where(at == place, table, 0), axis=0, keepdims=True)
        hit = (keys_ref[1] == column_row) & (keys_ref[0] == wanted)
        number = lax.broadcasted_iota(jnp.int32, (blocks, lanes), 0)
        picks[pl.ds(p, 1), :] = jnp.min(
            jnp.where(hit, number, blocks), axis=0, keepdims=True
        )
        return carry

    lax.fori_loop(0, rows, match, 0)
    for q in range(run):
        picks[pl.ds(rows + q, 1), :] = lbuf[row * run + q, 1:2, :]
    to_scalars = pltpu.make_async_copy(picks, pick_s, s_sem)
    to_scalars.start()
    to_scalars.wait()

    def share_copy(target_row, d, slot):
        return pltpu.make_async_remote_copy(
            src_ref=cbuf.at[target_row, d],
            dst_ref=pbuf.at[slot],
            send_sem=c_send.at[target_row, d],
            recv_sem=c_recv.at[slot],
            device_id=(target_row, col, d),
            device_id_type=MESH,
        )

    def start_share(target_row, d, slot):
        own = (target_row == row) & (depth == d)

        @pl.when(jnp.logical_not(own))
        def _():
            share_copy(target_row, d, slot).start()

        @pl.when(own)
        def _():
            pltpu.make_async_copy(cbuf.at[target_row, d], pbuf.at[slot], c_recv.at[slot]).start()

    def settle_share(target_row, d):
        @pl.when(jnp.logical_not((target_row == row) & (depth == d)))
        def _():
            share_copy(target_row, d, 0).wait_send()

    is_paired = functools.reduce(jnp.logical_or, [my_rel == rel for rel in paired], False)

    def mate_copy(t, target_row):
        return pltpu.make_async_remote_copy(
            src_ref=cbuf.at[target_row, 1 - depth],
            dst_ref=mbuf.at[t % 2],
            send_sem=m_send.at[t % 2],
            recv_sem=m_recv.at[t % 2],
            device_id=(row, col, 1 - depth),
            device_id_type=MESH,
        )

    @pl.when(active)
    def _():
        b_copy.wait()
        bbuf[blocks] = jnp.zeros(bbuf.shape[1:], bbuf.dtype)

        def one_run(t, carry):
            target_row = flip(col, n_row - 1 - t, n_row)

            def one_row(q, inner):
                p = target_row * run + q
                for rel in rels:

                    @pl.when(my_rel == rel)
                    def _(rel=rel):
                        part = a_part(abuf.at[p], rel)
                        pltpu.make_async_copy(part, part, a_recv.at[p]).wait()

                for u in range(0, targets, 2):
                    total = None
                    for v in range(0, width, 2):
                        left = jnp.concatenate([abuf[p, v], abuf[p, v + 1]], axis=1)
                        right = jnp.concatenate(
                            [
                                jnp.concatenate(
                                    [
                                        bbuf[pick_s[p, (v + i) * targets + u]],
                                        bbuf[pick_s[p, (v + i) * targets + u + 1]],
                                    ],
                                    axis=1,
                                )
                                for i in range(2)
                            ],
                            axis=0,
                        )
                        term = jnp.dot(left, right, preferred_element_type=jnp.float32)
                        total = term if total is None else total + term
                    edge = abuf.shape[-1]
                    for i in range(2):
                        cbuf[target_row, (u + i) // share, q, (u + i) % share] = total[
                            :, i * edge : (i + 1) * edge
                        ].astype(cbuf.dtype)
                return inner

            lax.fori_loop(0, run, one_row, 0)
            for rel in lone:

                @pl.when(my_rel == rel)
                def _(rel=rel):
                    for d in range(n_depth):
                        start_share(target_row, d, sender(rel))

            if paired:

                @pl.when(is_paired)
                def _():
                    @pl.when(t >= 2)
                    def _():
                        pl.semaphore_wait(m_free, 1)

                    exchange = mate_copy(t, target_row)
                    exchange.start()
                    exchange.wait()

                    def merge(q, inner):
                        for u in range(share):
                            cbuf[target_row, depth, q, u] = (
                                cbuf[target_row, depth, q, u].astype(jnp.float32)
                                + mbuf[t % 2, q, u].astype(jnp.float32)
                            ).astype(cbuf.dtype)
                        return inner

                    lax.fori_loop(0, run, merge, 0)

                    @pl.when(t < n_row - 2)
                    def _():
                        pl.semaphore_signal(
                            m_free,
                            inc=1,
                            device_id=(row, col, 1 - depth),
                            device_id_type=MESH,
                        )

                for slot, first in enumerate(senders):
                    if first in paired:

                        @pl.when(my_rel // 2 * 2 == first)
                        def _(slot=slot):
                            start_share(target_row, depth, slot)

            return carry

        lax.fori_loop(0, n_row, one_run, 0)

    for slot in range(len(senders)):
        pltpu.make_async_copy(pbuf.at[slot], pbuf.at[slot], c_recv.at[slot]).wait()

    def finish(i, carry):
        q = jnp.int32(0)
        for j in range(run):
            q = jnp.where(pick_s[rows + j, 0] == i, j, q)
        for u in range(share):
            value = pbuf[0, q, u].astype(jnp.float32)
            for slot in range(1, len(senders)):
                value = value + pbuf[slot, q, u].astype(jnp.float32)
            kept = keep_ref[i * share + u] > 0
            out_ref[i, u] = jnp.where(kept, value, jnp.float32(0.0)).astype(out_ref.dtype)
        return carry

    lax.fori_loop(0, run, finish, 0)

    sent = lbuf.at[pl.ds(0, rows - 1)]
    pltpu.make_async_copy(sent, sent, l_send).wait()
    for mine, remote in sends:
        @pl.when(jnp.logical_not(mine))
        def _(remote=remote):
            remote.wait_send()

    def settle(target_row, carry):
        for rel in lone:

            @pl.when(my_rel == rel)
            def _():
                for d in range(n_depth):
                    settle_share(target_row, d)

        if paired:

            @pl.when(is_paired)
            def _():
                settle_share(target_row, depth)

        return carry

    lax.fori_loop(0, n_row, settle, 0)


FIRST = (0xC0FCF0F0, 0xFFFFF0FC, 0x03F30303, 0xFFFFF0FC, 0x3F0FFFFF, 0xC0C0CFC0, 0x3F0FFFFF, 0x0F0F3F03)
STEPS = ((3, 1, 2, 0), (1, 3, 0, 2))


def bit(mask, index):
    word = jnp.int32(mask - (1 << 32) if mask >> 31 else mask)
    return lax.shift_right_logical(word, index) & 1


def torus_kernel(
    slots, held,
    pack_ref, keys_ref, keep_ref, a_ref, b_ref, out_ref,
    lbuf, picks, pick_s, abuf, bbuf, cbuf, mbuf, pbuf,
    l_send, l_recv, s_sem, b_sem, a_send, a_recv, f_send,
    m_send, m_recv, c_send, c_recv,
):
    n_row, n_col, n_depth = 4, 4, 2
    row, col, depth = (lax.axis_index(name) for name in ("row", "col", "depth"))
    run = n_col * n_depth
    rows = n_row * run
    me = (row * n_col + col) * n_depth + depth
    my_stripe = row * n_depth + depth
    blocks = b_ref.shape[0]
    share = pbuf.shape[2]
    targets = share * n_depth
    width = abuf.shape[1]
    half = width // 2
    edge = abuf.shape[-1]
    outer = flip_col(row, depth)
    is_main = col == row
    is_side = col == outer
    active = is_main | is_side
    my_edge = depth * half

    def list_copy(offset):
        dest = lax.rem(me + offset, rows)
        dest_row, dest_col, dest_depth = dest // run, dest // n_depth % n_col, dest % n_depth
        return pltpu.make_async_remote_copy(
            src_ref=pack_ref.at[dest_row * n_depth + dest_depth],
            dst_ref=lbuf.at[me],
            send_sem=l_send,
            recv_sem=l_recv,
            device_id=(dest_row, dest_col, dest_depth),
            device_id_type=MESH,
        )

    pltpu.make_async_copy(pack_ref.at[my_stripe], lbuf.at[me], l_recv).start()

    def send_list(offset, carry):
        list_copy(offset).start()
        return carry

    lax.fori_loop(1, rows, send_list, 0)

    b_copy = pltpu.make_async_copy(b_ref, bbuf.at[pl.ds(0, blocks)], b_sem)

    @pl.when(active)
    def _():
        b_copy.start()

    sends = []
    for t in range(n_col):
        c = flip(col, jnp.where(depth == 0, STEPS[0][t], STEPS[1][t]), n_col)
        for d in range(n_depth):
            s = c * n_depth + d
            first = jnp.int32(0)
            for panel in range(n_col):
                first = jnp.where(c == panel, bit(FIRST[panel * n_depth + d], me), first)
            for low, at_side in ((d * half, first), (half - d * half, jnp.int32(0))):
                dest_col = jnp.where(at_side == 1, flip_col(c, d), c)
                mine = (row == c) & (col == dest_col) & (depth == d)
                src = a_ref.at[pl.ds(s * width + low, half)]
                dst = abuf.at[me, pl.ds(low, half)]
                remote = pltpu.make_async_remote_copy(
                    src_ref=src,
                    dst_ref=dst,
                    send_sem=a_send.at[len(sends)],
                    recv_sem=a_recv.at[me],
                    device_id=(c, dest_col, d),
                    device_id_type=MESH,
                )
                local = pltpu.make_async_copy(src, dst, a_recv.at[me])
                sends.append((mine, remote))

                @pl.when(mine)
                def _(local=local):
                    local.start()

                @pl.when(jnp.logical_not(mine))
                def _(remote=remote):
                    remote.start()

    pltpu.make_async_copy(lbuf, lbuf, l_recv).wait()
    lanes = lbuf.shape[2]

    def match(p, carry):
        column_row = lbuf[p, 0:1, :]
        place = lbuf[p, 1:2, :]
        table = lbuf[(p // run * n_col + col) * n_depth, 8:, :]
        at = lax.broadcasted_iota(jnp.int32, (run, lanes), 0)
        wanted = jnp.sum(jnp.where(at == place, table, 0), axis=0, keepdims=True)
        hit = (keys_ref[1] == column_row) & (keys_ref[0] == wanted)
        number = lax.broadcasted_iota(jnp.int32, (blocks, lanes), 0)
        picks[pl.ds(p, 1), :] = jnp.min(
            jnp.where(hit, number, blocks), axis=0, keepdims=True
        )
        return carry

    lax.fori_loop(0, rows, match, 0)
    for q in range(run):
        picks[pl.ds(rows + q, 1), :] = lbuf[row * run + q, 1:2, :]
    to_scalars = pltpu.make_async_copy(picks, pick_s, s_sem)
    to_scalars.start()
    to_scalars.wait()

    my_first = [jnp.int32(0), jnp.int32(0)]

    def at_side_first(p):
        value = jnp.int32(0)
        for s in range(n_col * n_depth):
            value = jnp.where(my_stripe == s, bit(FIRST[s], p), value)
        return value

    def wait_blocks(p, count):
        part = abuf.at[p, pl.ds(0, count)]
        pltpu.make_async_copy(part, part, a_recv.at[p]).wait()

    def forward_copy(p, dest_col):
        part = abuf.at[p, pl.ds(my_edge, half)]
        return pltpu.make_async_remote_copy(
            src_ref=part,
            dst_ref=part,
            send_sem=f_send.at[p],
            recv_sem=a_recv.at[p],
            device_id=(row, dest_col, depth),
            device_id_type=MESH,
        )

    def batch_place(b):
        k, f = lax.rem(b, 2), b // 2
        step = jnp.int32(0)
        for t in range(n_col):
            step = jnp.where(f == t, jnp.where(k == 0, STEPS[0][t], STEPS[1][t]), step)
        return flip(row, step, n_col) * n_depth + k

    def arrivals(q, keep_first, count, dest_col):
        for j in range(n_row):
            p = j * run + q

            @pl.when(at_side_first(p) == keep_first)
            def _(p=p):
                wait_blocks(p, count)
                forward_copy(p, dest_col).start()

        for j in range(n_row):
            p = j * run + q

            @pl.when(at_side_first(p) != keep_first)
            def _(p=p):
                wait_blocks(p, count)

    def multiply(q, j, base, count):
        p = j * run + q
        left = jnp.concatenate([abuf[p, base + v] for v in range(count)], axis=1)
        for u in range(0, targets, 2):
            right = jnp.concatenate(
                [
                    jnp.concatenate(
                        [
                            bbuf[pick_s[p, (base + v) * targets + u]],
                            bbuf[pick_s[p, (base + v) * targets + u + 1]],
                        ],
                        axis=1,
                    )
                    for v in range(count)
                ],
                axis=0,
            )
            total = jnp.dot(left, right, preferred_element_type=jnp.float32)
            for i in range(2):
                cbuf[(u + i) // share, q, j, (u + i) % share] = total[
                    :, i * edge : (i + 1) * edge
                ].astype(cbuf.dtype)

    def share_copy(q, j, d, slot):
        return pltpu.make_async_remote_copy(
            src_ref=cbuf.at[d, q, j],
            dst_ref=pbuf.at[slot, q],
            send_sem=c_send,
            recv_sem=c_recv.at[slot],
            device_id=(j, col, d),
            device_id_type=MESH,
        )

    def start_share(q, j, d, slot):
        own = (row == j) & (depth == d)

        @pl.when(jnp.logical_not(own))
        def _():
            share_copy(q, j, d, slot).start()

        @pl.when(own)
        def _():
            pltpu.make_async_copy(cbuf.at[d, q, j], pbuf.at[slot, q], c_recv.at[slot]).start()

    def mate_copy(q):
        return pltpu.make_async_remote_copy(
            src_ref=cbuf.at[1 - depth, q],
            dst_ref=mbuf.at[q],
            send_sem=m_send,
            recv_sem=m_recv.at[q],
            device_id=(row, col, 1 - depth),
            device_id_type=MESH,
        )

    @pl.when(active)
    def _():
        b_copy.wait()
        bbuf[blocks] = jnp.zeros(bbuf.shape[1:], bbuf.dtype)

    @pl.when(is_main)
    def _():
        def one_batch(b, carry):
            @pl.when(b < run)
            def _():
                q = batch_place(b)
                arrivals(q, 0, width, outer)

                def one_row(j, inner):
                    multiply(q, j, 0, width)
                    return inner

                lax.fori_loop(0, n_row, one_row, 0)
                mate_copy(q).start()

            @pl.when(b > 0)
            def _():
                q = batch_place(b - 1)
                pltpu.make_async_copy(mbuf.at[q], mbuf.at[q], m_recv.at[q]).wait()

                def merge(j, inner):
                    for u in range(share):
                        cbuf[depth, q, j, u] = (
                            cbuf[depth, q, j, u].astype(jnp.float32)
                            + mbuf[q, j, u].astype(jnp.float32)
                        ).astype(cbuf.dtype)
                    return inner

                lax.fori_loop(0, n_row, merge, 0)
                for j in range(n_row):
                    start_share(q, j, depth, 0)

            return carry

        lax.fori_loop(0, run + 1, one_batch, 0)

    @pl.when(is_side)
    def _():
        def one_batch(b, carry):
            q = batch_place(b)
            arrivals(q, 1, half, row)

            def one_row(j, inner):
                multiply(q, j, my_edge, half)
                return inner

            lax.fori_loop(0, n_row, one_row, 0)
            for j in range(n_row):
                for d in range(n_depth):
                    start_share(q, j, d, 1 + depth)
            return carry

        lax.fori_loop(0, run, one_batch, 0)

    for slot in range(pbuf.shape[0]):
        pltpu.make_async_copy(pbuf.at[slot], pbuf.at[slot], c_recv.at[slot]).wait()

    def finish(i, carry):
        q = jnp.int32(0)
        for j in range(run):
            q = jnp.where(pick_s[rows + j, 0] == i, j, q)
        for u in range(share):
            value = pbuf[0, q, u].astype(jnp.float32)
            for slot in range(1, pbuf.shape[0]):
                value = value + pbuf[slot, q, u].astype(jnp.float32)
            kept = keep_ref[i * share + u] > 0
            out_ref[i, u] = jnp.where(kept, value, jnp.float32(0.0)).astype(out_ref.dtype)
        return carry

    lax.fori_loop(0, run, finish, 0)

    sent = lbuf.at[pl.ds(0, rows - 1)]
    pltpu.make_async_copy(sent, sent, l_send).wait()
    for mine, remote in sends:

        @pl.when(jnp.logical_not(mine))
        def _(remote=remote):
            remote.wait_send()

    def settle_forwards(keep_first, dest_col):
        def settle(p, carry):
            @pl.when(at_side_first(p) == keep_first)
            def _():
                forward_copy(p, dest_col).wait_send()

            return carry

        lax.fori_loop(0, rows, settle, 0)

    @pl.when(is_main)
    def _():
        settle_forwards(0, outer)
        pltpu.make_async_copy(mbuf, mbuf, m_send).wait()
        part = cbuf.at[0, :, pl.ds(0, n_row - 1)]
        pltpu.make_async_copy(part, part, c_send).wait()

    @pl.when(is_side)
    def _():
        settle_forwards(1, row)
        part = cbuf.at[:, :, pl.ds(0, n_row - 1)]
        pltpu.make_async_copy(part, part, c_send).wait()
        part = cbuf.at[0, :, 0]
        pltpu.make_async_copy(part, part, c_send).wait()


def flip_col(column, depth):
    return lax.rem(column + 2 * depth - 1 + 4, 4)


def on_device(
    a_blocks, a_columns, a_live, atom_rows, b_blocks, b_columns, b_live, c_columns, c_live
):
    n_row, n_col, n_depth = (lax.axis_size(name) for name in ("row", "col", "depth"))
    row, depth = (lax.axis_index(name) for name in ("row", "depth"))
    _, group_count, slots = a_columns.shape
    edge = a_blocks.shape[-1]
    stripe, _, list_width = b_columns.shape
    run, _, targets = c_columns.shape
    stripes = n_row * n_depth
    total = stripe * stripes
    share = targets // n_depth
    width = group_count * slots // stripes
    row_count = n_row * run
    kinds = stripe_kinds(total, stripe, total // n_col)
    senders = {rel // 2 * 2 if rel ^ 1 in kinds and n_depth == 2 else rel for rel in kinds}
    block_count = stripe * list_width
    lanes = -(-width * targets // 128) * 128
    spare = lanes - width * targets

    firsts = jnp.arange(stripes, dtype=jnp.int32)[:, None] * stripe
    a_keys = jnp.where(a_live > 0, a_columns, -total).reshape(stripes, width) - firsts
    a_keys = jnp.repeat(a_keys, targets, axis=1)
    a_keys = jnp.pad(a_keys, ((0, 0), (0, spare)), constant_values=-1)[:, None]
    place = jnp.broadcast_to((atom_rows - row * run).reshape(1, 1, 1), (stripes, 1, lanes))
    table = jnp.tile(c_columns[:, 0, :], (1, width))
    table = jnp.pad(table, ((0, 0), (0, spare)), constant_values=-2)
    pack = jnp.concatenate(
        [
            a_keys,
            place,
            jnp.zeros((stripes, 6, lanes), jnp.int32),
            jnp.broadcast_to(table[None], (stripes, run, lanes)),
        ],
        axis=1,
    )
    b_keys = jnp.where(b_live > 0, b_columns, -1).reshape(-1)
    b_rows = jnp.arange(block_count, dtype=jnp.int32) // list_width
    keys = jnp.broadcast_to(jnp.stack([b_keys, b_rows])[:, :, None], (2, block_count, lanes))
    keep = lax.dynamic_slice_in_dim(c_live[:, 0, :], depth * share, share, 1).reshape(-1)

    operands = (pack, keys, keep, a_blocks.reshape(-1, edge, edge), b_blocks.reshape(-1, edge, edge))
    lists = [
        pltpu.VMEM((row_count, 8 + run, lanes), jnp.int32),
        pltpu.VMEM((row_count + run, lanes), jnp.int32),
        pltpu.SMEM((row_count + run, lanes), jnp.int32),
        pltpu.VMEM((row_count, width, edge, edge), jnp.bfloat16),
        pltpu.VMEM((block_count + 1, edge, edge), jnp.bfloat16),
    ]
    if (n_row, n_col, n_depth) == (4, 4, 2) and sorted(kinds) == [0, 1, 2, 7]:
        body = functools.partial(torus_kernel, slots, kinds)
        scratch = lists + [
            pltpu.VMEM((n_depth, run, n_row, share, edge, edge), jnp.bfloat16),
            pltpu.VMEM((run, n_row, share, edge, edge), jnp.bfloat16),
            pltpu.VMEM((3, run, share, edge, edge), jnp.bfloat16),
            pltpu.SemaphoreType.DMA,
            pltpu.SemaphoreType.DMA,
            pltpu.SemaphoreType.DMA,
            pltpu.SemaphoreType.DMA,
            pltpu.SemaphoreType.DMA((2 * n_col * n_depth,)),
            pltpu.SemaphoreType.DMA((row_count,)),
            pltpu.SemaphoreType.DMA((row_count,)),
            pltpu.SemaphoreType.DMA,
            pltpu.SemaphoreType.DMA((run,)),
            pltpu.SemaphoreType.DMA,
            pltpu.SemaphoreType.DMA((3,)),
        ]
    else:
        body = functools.partial(kernel, n_row, n_col, n_depth, kinds, slots)
        scratch = lists + [
            pltpu.VMEM((n_row, n_depth, run, share, edge, edge), jnp.bfloat16),
            pltpu.VMEM((2, run, share, edge, edge), jnp.bfloat16),
            pltpu.VMEM((len(senders), run, share, edge, edge), jnp.bfloat16),
            pltpu.SemaphoreType.DMA,
            pltpu.SemaphoreType.DMA,
            pltpu.SemaphoreType.DMA,
            pltpu.SemaphoreType.DMA,
            pltpu.SemaphoreType.DMA((n_col * len(kinds),)),
            pltpu.SemaphoreType.DMA((row_count,)),
            pltpu.SemaphoreType.DMA((2,)),
            pltpu.SemaphoreType.DMA((2,)),
            pltpu.SemaphoreType.REGULAR,
            pltpu.SemaphoreType.DMA((n_row, n_depth)),
            pltpu.SemaphoreType.DMA((len(senders),)),
        ]
    result = pl.pallas_call(
        body,
        out_shape=jax.ShapeDtypeStruct((run, share, edge, edge), jnp.bfloat16),
        in_specs=[
            pl.BlockSpec(memory_space=pltpu.VMEM),
            pl.BlockSpec(memory_space=pltpu.VMEM),
            pl.BlockSpec(memory_space=pltpu.SMEM),
            pl.BlockSpec(memory_space=pl.ANY),
            pl.BlockSpec(memory_space=pl.ANY),
        ],
        out_specs=pl.BlockSpec(memory_space=pltpu.VMEM),
        scratch_shapes=scratch,
        compiler_params=pltpu.CompilerParams(
            has_side_effects=True, vmem_limit_bytes=60 * 1024 * 1024
        ),
    )(*operands)
    return result[:, None]


def solution(mesh):
    placed = (
        P(("row", "col", "depth"), None, None, None, None),
        P(("row", "col", "depth"), None, None),
        P(("row", "col", "depth"), None, None),
        P(("row", "col", "depth")),
        P(("row", "depth"), "col", None, None, None),
        P(("row", "depth"), "col", None),
        P(("row", "depth"), "col", None),
        P("row", "col", None),
        P("row", "col", None),
    )
    return jax.shard_map(
        on_device,
        mesh=mesh,
        in_specs=placed,
        out_specs=P("row", "col", "depth", None, None),
        check_vma=False,
    )
```

```python
import functools

import jax
import jax.numpy as jnp
from jax import lax
from jax.experimental import pallas as pl
from jax.experimental.pallas import tpu as pltpu
from jax.sharding import PartitionSpec as P

GW = 10
REACH = 16
MESH = pl.DeviceIdType.MESH


def stripe_kinds(total, stripe, panel):
    kinds = {}
    for rel in range(total // stripe):
        groups = []
        for g in range(stripe // GW):
            first = rel * stripe + g * GW
            if any((k + REACH) % total < panel + 2 * REACH for k in range(first, first + GW)):
                groups.append(g)
        if groups:
            kinds[rel] = (groups[0], groups[-1] + 1)
    return kinds


def flip(index, step, count):
    return lax.rem(index // 2 + step // 2, count // 2) * 2 + lax.rem(index + step, 2)


def kernel(
    n_row, n_col, n_depth, kinds, slots,
    pack_ref, keys_ref, keep_ref, a_ref, b_ref, out_ref,
    lbuf, picks, pick_s, abuf, bbuf, cbuf, mbuf, pbuf,
    l_send, l_recv, s_sem, b_sem, a_send, a_recv, m_send, m_recv, m_free, c_send, c_recv,
):
    row, col, depth = (lax.axis_index(name) for name in ("row", "col", "depth"))
    stripes = n_row * n_depth
    per_panel = stripes // n_col
    run = n_col * n_depth
    rows = n_row * run
    me = (row * n_col + col) * n_depth + depth
    my_stripe = row * n_depth + depth
    my_rel = lax.rem(my_stripe - per_panel * col + stripes, stripes)
    rels = sorted(kinds)
    blocks = b_ref.shape[0]
    share = pbuf.shape[2]
    targets = share * n_depth
    width = a_ref.shape[0] // stripes
    groups = width // slots
    active = functools.reduce(jnp.logical_or, [my_rel == rel for rel in rels])
    paired = [rel for rel in rels if rel ^ 1 in kinds and n_depth == 2]
    lone = [rel for rel in rels if rel not in paired]
    senders = sorted({rel // 2 * 2 if rel in paired else rel for rel in rels})

    def sender(rel):
        return senders.index(rel // 2 * 2 if rel in paired else rel)

    def a_part(ref, rel):
        low, high = kinds[rel]
        return ref.at[pl.ds(low * slots, (high - low) * slots)]

    def list_copy(offset):
        dest = lax.rem(me + offset, rows)
        dest_row, dest_col, dest_depth = dest // run, dest // n_depth % n_col, dest % n_depth
        return pltpu.make_async_remote_copy(
            src_ref=pack_ref.at[dest_row * n_depth + dest_depth],
            dst_ref=lbuf.at[me],
            send_sem=l_send,
            recv_sem=l_recv,
            device_id=(dest_row, dest_col, dest_depth),
            device_id_type=MESH,
        )

    pltpu.make_async_copy(pack_ref.at[my_stripe], lbuf.at[me], l_recv).start()

    def send_list(offset, carry):
        list_copy(offset).start()
        return carry

    lax.fori_loop(1, rows, send_list, 0)

    b_copy = pltpu.make_async_copy(b_ref, bbuf.at[pl.ds(0, blocks)], b_sem)

    @pl.when(active)
    def _():
        b_copy.start()

    sends = []
    for t in reversed(range(n_col)):
        c = flip(row, t, n_col)
        for rel in rels:
            s = lax.rem(per_panel * c + rel, stripes)
            low, high = kinds[rel]
            src = a_ref.at[pl.ds(s * width + low * slots, (high - low) * slots)]
            mine = (my_stripe == s) & (col == c)
            remote = pltpu.make_async_remote_copy(
                src_ref=src,
                dst_ref=a_part(abuf.at[me], rel),
                send_sem=a_send.at[len(sends)],
                recv_sem=a_recv.at[me],
                device_id=(s // n_depth, c, s % n_depth),
                device_id_type=MESH,
            )
            local = pltpu.make_async_copy(src, a_part(abuf.at[me], rel), a_recv.at[me])
            sends.append((mine, remote))

            @pl.when(mine)
            def _(local=local):
                local.start()

            @pl.when(jnp.logical_not(mine))
            def _(remote=remote):
                remote.start()

    for rel in rels:
        low, high = kinds[rel]
        gaps = [g for g in range(groups) if not low <= g < high]
        if gaps:

            @pl.when(my_rel == rel)
            def _(gaps=gaps):
                def clear(p, carry):
                    for g in gaps:
                        for v in range(g * slots, (g + 1) * slots):
                            abuf[p, v] = jnp.zeros(abuf.shape[2:], abuf.dtype)
                    return carry

                lax.fori_loop(0, rows, clear, 0)

    pltpu.make_async_copy(lbuf, lbuf, l_recv).wait()
    lanes = lbuf.shape[2]

    def match(p, carry):
        column_row = lbuf[p, 0:1, :]
        place = lbuf[p, 1:2, :]
        table = lbuf[(p // run * n_col + col) * n_depth, 8:, :]
        at = lax.broadcasted_iota(jnp.int32, (run, lanes), 0)
        wanted = jnp.sum(jnp.where(at == place, table, 0), axis=0, keepdims=True)
        hit = (keys_ref[1] == column_row) & (keys_ref[0] == wanted)
        number = lax.broadcasted_iota(jnp.int32, (blocks, lanes), 0)
        picks[pl.ds(p, 1), :] = jnp.min(
            jnp.where(hit, number, blocks), axis=0, keepdims=True
        )
        return carry

    lax.fori_loop(0, rows, match, 0)
    for q in range(run):
        picks[pl.ds(rows + q, 1), :] = lbuf[row * run + q, 1:2, :]
    to_scalars = pltpu.make_async_copy(picks, pick_s, s_sem)
    to_scalars.start()
    to_scalars.wait()

    def share_copy(target_row, d, slot):
        return pltpu.make_async_remote_copy(
            src_ref=cbuf.at[target_row, d],
            dst_ref=pbuf.at[slot],
            send_sem=c_send.at[target_row, d],
            recv_sem=c_recv.at[slot],
            device_id=(target_row, col, d),
            device_id_type=MESH,
        )

    def start_share(target_row, d, slot):
        own = (target_row == row) & (depth == d)

        @pl.when(jnp.logical_not(own))
        def _():
            share_copy(target_row, d, slot).start()

        @pl.when(own)
        def _():
            pltpu.make_async_copy(cbuf.at[target_row, d], pbuf.at[slot], c_recv.at[slot]).start()

    def settle_share(target_row, d):
        @pl.when(jnp.logical_not((target_row == row) & (depth == d)))
        def _():
            share_copy(target_row, d, 0).wait_send()

    is_paired = functools.reduce(jnp.logical_or, [my_rel == rel for rel in paired], False)

    def mate_copy(t, target_row):
        return pltpu.make_async_remote_copy(
            src_ref=cbuf.at[target_row, 1 - depth],
            dst_ref=mbuf.at[t % 2],
            send_sem=m_send.at[t % 2],
            recv_sem=m_recv.at[t % 2],
            device_id=(row, col, 1 - depth),
            device_id_type=MESH,
        )

    @pl.when(active)
    def _():
        b_copy.wait()
        bbuf[blocks] = jnp.zeros(bbuf.shape[1:], bbuf.dtype)

        def one_run(t, carry):
            target_row = flip(col, n_row - 1 - t, n_row)

            def one_row(q, inner):
                p = target_row * run + q
                for rel in rels:

                    @pl.when(my_rel == rel)
                    def _(rel=rel):
                        part = a_part(abuf.at[p], rel)
                        pltpu.make_async_copy(part, part, a_recv.at[p]).wait()

                for u in range(0, targets, 2):
                    total = None
                    for v in range(0, width, 2):
                        left = jnp.concatenate([abuf[p, v], abuf[p, v + 1]], axis=1)
                        right = jnp.concatenate(
                            [
                                jnp.concatenate(
                                    [
                                        bbuf[pick_s[p, (v + i) * targets + u]],
                                        bbuf[pick_s[p, (v + i) * targets + u + 1]],
                                    ],
                                    axis=1,
                                )
                                for i in range(2)
                            ],
                            axis=0,
                        )
                        term = jnp.dot(left, right, preferred_element_type=jnp.float32)
                        total = term if total is None else total + term
                    edge = abuf.shape[-1]
                    for i in range(2):
                        cbuf[target_row, (u + i) // share, q, (u + i) % share] = total[
                            :, i * edge : (i + 1) * edge
                        ].astype(cbuf.dtype)
                return inner

            lax.fori_loop(0, run, one_row, 0)
            for rel in lone:

                @pl.when(my_rel == rel)
                def _(rel=rel):
                    for d in range(n_depth):
                        start_share(target_row, d, sender(rel))

            if paired:

                @pl.when(is_paired)
                def _():
                    @pl.when(t >= 2)
                    def _():
                        pl.semaphore_wait(m_free, 1)

                    exchange = mate_copy(t, target_row)
                    exchange.start()
                    exchange.wait()

                    def merge(q, inner):
                        for u in range(share):
                            cbuf[target_row, depth, q, u] = (
                                cbuf[target_row, depth, q, u].astype(jnp.float32)
                                + mbuf[t % 2, q, u].astype(jnp.float32)
                            ).astype(cbuf.dtype)
                        return inner

                    lax.fori_loop(0, run, merge, 0)

                    @pl.when(t < n_row - 2)
                    def _():
                        pl.semaphore_signal(
                            m_free,
                            inc=1,
                            device_id=(row, col, 1 - depth),
                            device_id_type=MESH,
                        )

                for slot, first in enumerate(senders):
                    if first in paired:

                        @pl.when(my_rel // 2 * 2 == first)
                        def _(slot=slot):
                            start_share(target_row, depth, slot)

            return carry

        lax.fori_loop(0, n_row, one_run, 0)

    for slot in range(len(senders)):
        pltpu.make_async_copy(pbuf.at[slot], pbuf.at[slot], c_recv.at[slot]).wait()

    def finish(i, carry):
        q = jnp.int32(0)
        for j in range(run):
            q = jnp.where(pick_s[rows + j, 0] == i, j, q)
        for u in range(share):
            value = pbuf[0, q, u].astype(jnp.float32)
            for slot in range(1, len(senders)):
                value = value + pbuf[slot, q, u].astype(jnp.float32)
            kept = keep_ref[i * share + u] > 0
            out_ref[i, u] = jnp.where(kept, value, jnp.float32(0.0)).astype(out_ref.dtype)
        return carry

    lax.fori_loop(0, run, finish, 0)

    sent = lbuf.at[pl.ds(0, rows - 1)]
    pltpu.make_async_copy(sent, sent, l_send).wait()
    for mine, remote in sends:
        @pl.when(jnp.logical_not(mine))
        def _(remote=remote):
            remote.wait_send()

    def settle(target_row, carry):
        for rel in lone:

            @pl.when(my_rel == rel)
            def _():
                for d in range(n_depth):
                    settle_share(target_row, d)

        if paired:

            @pl.when(is_paired)
            def _():
                settle_share(target_row, depth)

        return carry

    lax.fori_loop(0, n_row, settle, 0)


BY_MAIN_FIRST, VIA_RELAY, DIRECT = 0, 1, 2
ORDER = (
    0x17543206, 0x54107632, 0x37261054, 0x73645210, 0x54701632, 0x43620751, 0x76325410, 0x32761054,
    0x47061235, 0x1432567, 0x32760451, 0x61274530, 0x45137602, 0x73014625, 0x34762510, 0x2745361,
    0x75032416, 0x43015267, 0x4763152, 0x32640175, 0x16503247, 0x45017326, 0x76345210, 0x30716542,
    0x10543276, 0x54107632, 0x34157026, 0x23076145, 0x4132567, 0x40516723, 0x76325410, 0x60234571,
)
ROUTES = (
    0x5510, 0x5510, 0x1505, 0x9509, 0x1165, 0x1145, 0x546, 0x2545,
    0x5120, 0x5118, 0x5104, 0x5100, 0x5049, 0x5081, 0x2441, 0x2441,
    0x4118, 0x4118, 0x4205, 0x6105, 0x45, 0x1045, 0x2445, 0x845,
    0x5158, 0x9150, 0x5144, 0x5944, 0x6056, 0x5054, 0x455, 0x455,
)
BY_MAIN = (
    0x2f030f03, 0x200e903, 0xcfcfcec, 0xf0f0f, 0xf0f0f000, 0x373f3f30, 0xc0970040, 0xc0f0c0f4,
)
RELAYED = (
    (7, 3, 12, 14, 22, 23, 30, 31, 15, 13, 4, 19, 20, 5, 21, 2, 18),
    (2, 10, 5, 18, 19, 26, 31, 27, 6, 22, 30, 4, 23, 29, 28, 7, 21, 20),
    (9, 0, 1, 16, 24, 25, 28, 17, 29, 30, 31),
    (12, 4, 20, 28, 29, 21, 5, 25, 15, 27, 26, 24, 31, 30, 7, 23, 6, 14, 22),
    (19, 27, 2, 3, 7, 11, 10, 26, 6, 16, 5, 4, 0, 1, 25, 24, 8, 9, 17),
    (22, 31, 6, 7, 15, 3, 30, 14, 2, 0, 1),
    (29, 21, 24, 26, 0, 5, 12, 13, 4, 9, 1, 27, 25, 8, 2, 3, 10, 11),
    (24, 28, 8, 9, 17, 19, 0, 1, 16, 18, 27, 11, 12, 26, 10, 29, 13),
)
MAIN_ROWS = (
    (0, 1, 10, 8, 9, 11, 26, 27, 16, 17, 24, 25, 29, 28, 6, 7, 3, 12, 14, 22, 23, 30, 31, 15, 13, 4, 19, 20, 5, 21, 2, 18),
    (10, 11, 2, 3, 12, 13, 4, 20, 21, 18, 19, 5, 15, 26, 27, 8, 6, 9, 23, 0, 7, 1, 22, 16, 14, 24, 25, 28, 17, 29, 30, 31),
    (20, 21, 28, 29, 18, 19, 27, 12, 13, 11, 10, 26, 16, 5, 4, 25, 22, 24, 23, 8, 31, 9, 6, 17, 7, 15, 3, 30, 14, 2, 0, 1),
    (30, 31, 21, 22, 23, 20, 5, 4, 6, 7, 14, 15, 2, 3, 24, 25, 28, 8, 9, 17, 19, 0, 1, 16, 18, 27, 11, 12, 26, 10, 29, 13),
)
SIDE_ROWS = (
    (6, 7, 3, 12, 14, 22, 23, 30, 31, 15, 28, 13, 4, 19, 20, 5, 21, 2, 18, 0, 1, 10, 8, 9, 11, 26, 27, 16, 17, 24, 25, 29),
    (2, 3, 10, 18, 19, 26, 31, 27, 6, 5, 22, 30, 4, 12, 29, 28, 7, 17, 23, 21, 20, 24, 0, 1, 9, 8, 11, 16, 25, 14, 15, 13),
    (8, 9, 0, 1, 4, 16, 24, 25, 28, 17, 29, 10, 11, 2, 3, 12, 30, 13, 20, 21, 18, 19, 31, 5, 15, 26, 27, 6, 23, 7, 22, 14),
    (12, 13, 4, 20, 28, 29, 21, 5, 25, 15, 26, 27, 24, 31, 30, 6, 23, 7, 10, 11, 22, 2, 14, 3, 18, 19, 8, 9, 0, 1, 16, 17),
    (18, 19, 27, 2, 3, 7, 11, 10, 26, 6, 16, 5, 0, 4, 25, 1, 24, 8, 20, 9, 21, 17, 28, 29, 12, 13, 22, 23, 31, 15, 30, 14),
    (22, 23, 27, 31, 6, 7, 15, 3, 30, 14, 2, 20, 21, 28, 29, 18, 19, 12, 13, 11, 10, 26, 0, 1, 16, 5, 4, 25, 24, 8, 9, 17),
    (28, 29, 21, 24, 0, 5, 12, 13, 4, 9, 26, 1, 27, 19, 25, 2, 3, 14, 7, 8, 10, 11, 30, 31, 23, 20, 22, 6, 15, 17, 16, 18),
    (24, 25, 28, 8, 9, 17, 19, 0, 1, 16, 3, 18, 27, 11, 12, 26, 10, 29, 13, 30, 31, 21, 22, 23, 20, 5, 4, 6, 7, 14, 15, 2),
)


def pick_word(words, index):
    value = jnp.int32(0)
    for i, word in enumerate(words):
        word = jnp.int32(word - (1 << 32) if word >> 31 else word)
        value = jnp.where(index == i, word, value)
    return value


def field(word, index, bits):
    return lax.shift_right_logical(word, index * bits) & ((1 << bits) - 1)


def torus_kernel(
    slots, held,
    pack_ref, keys_ref, keep_ref, a_ref, b_ref, out_ref,
    lbuf, picks, pick_s, abuf, bbuf, cbuf, mbuf, pbuf,
    l_send, l_recv, s_sem, b_sem, a_send, a_recv, f_send,
    m_send, m_recv, c_send, c_recv,
):
    n_row, n_col, n_depth = 4, 4, 2
    row, col, depth = (lax.axis_index(name) for name in ("row", "col", "depth"))
    run = n_col * n_depth
    rows = n_row * run
    me = (row * n_col + col) * n_depth + depth
    my_stripe = row * n_depth + depth
    blocks = b_ref.shape[0]
    share = pbuf.shape[2]
    targets = share * n_depth
    width = abuf.shape[1]
    half = width // 2
    edge = abuf.shape[-1]
    outer = side_col(row, depth)
    is_main = col == row
    is_side = col == outer
    is_relay = col == side_col(row, 1 - depth)
    active = is_main | is_side
    my_edge = depth * half

    def list_copy(offset):
        dest = lax.rem(me + offset, rows)
        dest_row, dest_col, dest_depth = dest // run, dest // n_depth % n_col, dest % n_depth
        return pltpu.make_async_remote_copy(
            src_ref=pack_ref.at[dest_row * n_depth + dest_depth],
            dst_ref=lbuf.at[me],
            send_sem=l_send,
            recv_sem=l_recv,
            device_id=(dest_row, dest_col, dest_depth),
            device_id_type=MESH,
        )

    pltpu.make_async_copy(pack_ref.at[my_stripe], lbuf.at[me], l_recv).start()

    def send_list(offset, carry):
        list_copy(offset).start()
        return carry

    lax.fori_loop(1, rows, send_list, 0)

    b_copy = pltpu.make_async_copy(b_ref, bbuf.at[pl.ds(0, blocks)], b_sem)

    @pl.when(active)
    def _():
        b_copy.start()

    sends = []

    def send_part(wanted, src, low, place):
        mine = (row == place[0]) & (col == place[1]) & (depth == place[2])
        dst = abuf.at[me, pl.ds(low, half)]
        remote = pltpu.make_async_remote_copy(
            src_ref=src,
            dst_ref=dst,
            send_sem=a_send.at[len(sends)],
            recv_sem=a_recv.at[me],
            device_id=place,
            device_id_type=MESH,
        )
        local = pltpu.make_async_copy(src, dst, a_recv.at[me])
        away = wanted & jnp.logical_not(mine)
        sends.append((away, remote))

        @pl.when(wanted & mine)
        def _():
            local.start()

        @pl.when(away)
        def _():
            remote.start()

    my_order = pick_word(ORDER, me)
    my_routes = pick_word(ROUTES, me)
    always = me >= 0
    for t in range(n_col * n_depth):
        s = field(my_order, t, 4)
        c, d = s // n_depth, s % n_depth
        route = field(my_routes, s, 2)
        side = side_col(c, d)
        edge_low, mid_low = d * half, half - d * half
        edge_src = a_ref.at[pl.ds(s * width + edge_low, half)]
        mid_src = a_ref.at[pl.ds(s * width + mid_low, half)]
        via = route == VIA_RELAY
        send_part(
            always,
            edge_src,
            edge_low,
            (c, jnp.where(via, side, c), jnp.where(via, 1 - d, d)),
        )
        send_part(route == DIRECT, edge_src, edge_low, (c, side, d))
        send_part(always, mid_src, mid_low, (c, c, d))

    far_edge = (1 - depth) * half

    def relay_copy(p, dest_col):
        part = abuf.at[p, pl.ds(far_edge, half)]
        return pltpu.make_async_remote_copy(
            src_ref=part,
            dst_ref=part,
            send_sem=f_send.at[p],
            recv_sem=a_recv.at[p],
            device_id=(row, dest_col, 1 - depth),
            device_id_type=MESH,
        )

    def wait_blocks(p, count):
        part = abuf.at[p, pl.ds(0, count)]
        pltpu.make_async_copy(part, part, a_recv.at[p]).wait()

    other_stripe = row * n_depth + 1 - depth
    relayed_rows = pick_word([len(r) for r in RELAYED], other_stripe)
    relay_words = [
        pick_word([pack_bytes(r)[w] for r in RELAYED], other_stripe) for w in range(rows // 4)
    ]

    def table_row(words, i):
        word = words[0]
        for w in range(1, len(words)):
            word = jnp.where(i // 4 == w, words[w], word)
        return field(word, i % 4, 8)

    @pl.when(is_relay)
    def _():
        def relay(i, carry):
            p = table_row(relay_words, i)
            wait_blocks(p, half)
            relay_copy(p, row).start()
            relay_copy(p, col).start()
            return carry

        lax.fori_loop(0, relayed_rows, relay, 0)

    pltpu.make_async_copy(lbuf, lbuf, l_recv).wait()
    lanes = lbuf.shape[2]

    def match(p, carry):
        column_row = lbuf[p, 0:1, :]
        place = lbuf[p, 1:2, :]
        table = lbuf[(p // run * n_col + col) * n_depth, 8:, :]
        at = lax.broadcasted_iota(jnp.int32, (run, lanes), 0)
        wanted = jnp.sum(jnp.where(at == place, table, 0), axis=0, keepdims=True)
        hit = (keys_ref[1] == column_row) & (keys_ref[0] == wanted)
        number = lax.broadcasted_iota(jnp.int32, (blocks, lanes), 0)
        picks[pl.ds(p, 1), :] = jnp.min(
            jnp.where(hit, number, blocks), axis=0, keepdims=True
        )
        return carry

    lax.fori_loop(0, rows, match, 0)
    for q in range(run):
        picks[pl.ds(rows + q, 1), :] = lbuf[row * run + q, 1:2, :]
    to_scalars = pltpu.make_async_copy(picks, pick_s, s_sem)
    to_scalars.start()
    to_scalars.wait()

    main_words = [pick_word([pack_bytes(r)[w] for r in MAIN_ROWS], row) for w in range(run)]
    side_words = [pick_word([pack_bytes(r)[w] for r in SIDE_ROWS], my_stripe) for w in range(run)]
    by_main = pick_word(BY_MAIN, my_stripe)

    def forward_copy(p, dest_col):
        part = abuf.at[p, pl.ds(my_edge, half)]
        return pltpu.make_async_remote_copy(
            src_ref=part,
            dst_ref=part,
            send_sem=f_send.at[p],
            recv_sem=a_recv.at[p],
            device_id=(row, dest_col, depth),
            device_id_type=MESH,
        )

    def batch_rows(words, b):
        word = words[0]
        for w in range(1, len(words)):
            word = jnp.where(b == w, words[w], word)
        return [field(word, i, 8) for i in range(n_row)]

    def multiply(p, b, at, base, count):
        left = jnp.concatenate([abuf[p, base + v] for v in range(count)], axis=1)
        for u in range(0, targets, 2):
            right = jnp.concatenate(
                [
                    jnp.concatenate(
                        [
                            bbuf[pick_s[p, (base + v) * targets + u]],
                            bbuf[pick_s[p, (base + v) * targets + u + 1]],
                        ],
                        axis=1,
                    )
                    for v in range(count)
                ],
                axis=0,
            )
            total = jnp.dot(left, right, preferred_element_type=jnp.float32)
            for i in range(2):
                cbuf[(u + i) // share, b, at, (u + i) % share] = total[
                    :, i * edge : (i + 1) * edge
                ].astype(cbuf.dtype)

    def start_share(p, b, at, d, slot):
        target, q = p // run, p % run
        own = (row == target) & (depth == d)
        src = cbuf.at[d, b, at]
        dst = pbuf.at[slot, q]

        @pl.when(jnp.logical_not(own))
        def _():
            pltpu.make_async_remote_copy(
                src_ref=src,
                dst_ref=dst,
                send_sem=c_send,
                recv_sem=c_recv.at[slot],
                device_id=(target, col, d),
                device_id_type=MESH,
            ).start()

        @pl.when(own)
        def _():
            pltpu.make_async_copy(src, dst, c_recv.at[slot]).start()

    def mate_copy(b):
        return pltpu.make_async_remote_copy(
            src_ref=cbuf.at[1 - depth, b],
            dst_ref=mbuf.at[b],
            send_sem=m_send,
            recv_sem=m_recv.at[b],
            device_id=(row, col, 1 - depth),
            device_id_type=MESH,
        )

    @pl.when(active)
    def _():
        b_copy.wait()
        bbuf[blocks] = jnp.zeros(bbuf.shape[1:], bbuf.dtype)

    @pl.when(is_main)
    def _():
        def one_batch(b, carry):
            @pl.when(b < run)
            def _():
                members = batch_rows(main_words, b)
                for p in members:

                    @pl.when(field(by_main, p, 1) == 1)
                    def _(p=p):
                        wait_blocks(p, width)
                        forward_copy(p, outer).start()

                for p in members:

                    @pl.when(field(by_main, p, 1) == 0)
                    def _(p=p):
                        wait_blocks(p, width)

                def one_row(i, inner):
                    multiply(table_row(main_words, b * n_row + i), b, i, 0, width)
                    return inner

                lax.fori_loop(0, n_row, one_row, 0)
                mate_copy(b).start()

            @pl.when(b > 0)
            def _():
                last = b - 1
                pltpu.make_async_copy(mbuf.at[last], mbuf.at[last], m_recv.at[last]).wait()

                def merge(i, inner):
                    for u in range(share):
                        cbuf[depth, last, i, u] = (
                            cbuf[depth, last, i, u].astype(jnp.float32)
                            + mbuf[last, i, u].astype(jnp.float32)
                        ).astype(cbuf.dtype)
                    return inner

                lax.fori_loop(0, n_row, merge, 0)
                for i, p in enumerate(batch_rows(main_words, last)):
                    start_share(p, last, i, depth, 0)

            return carry

        lax.fori_loop(0, run + 1, one_batch, 0)

    @pl.when(is_side)
    def _():
        def one_batch(b, carry):
            members = batch_rows(side_words, b)
            for p in members:
                wait_blocks(p, half)

            def one_row(i, inner):
                multiply(table_row(side_words, b * n_row + i), b, i, my_edge, half)
                return inner

            lax.fori_loop(0, n_row, one_row, 0)
            for i, p in enumerate(members):
                for d in range(n_depth):
                    start_share(p, b, i, d, 1 + depth)
            return carry

        lax.fori_loop(0, run, one_batch, 0)

    for slot in range(pbuf.shape[0]):
        pltpu.make_async_copy(pbuf.at[slot], pbuf.at[slot], c_recv.at[slot]).wait()

    def finish(i, carry):
        q = jnp.int32(0)
        for j in range(run):
            q = jnp.where(pick_s[rows + j, 0] == i, j, q)
        for u in range(share):
            value = pbuf[0, q, u].astype(jnp.float32)
            for slot in range(1, pbuf.shape[0]):
                value = value + pbuf[slot, q, u].astype(jnp.float32)
            kept = keep_ref[i * share + u] > 0
            out_ref[i, u] = jnp.where(kept, value, jnp.float32(0.0)).astype(out_ref.dtype)
        return carry

    lax.fori_loop(0, run, finish, 0)

    sent = lbuf.at[pl.ds(0, rows - 1)]
    pltpu.make_async_copy(sent, sent, l_send).wait()
    for away, remote in sends:

        @pl.when(away)
        def _(remote=remote):
            remote.wait_send()

    @pl.when(is_relay)
    def _():
        def settle(i, carry):
            part = abuf.at[0]
            pltpu.make_async_copy(part, part, f_send.at[table_row(relay_words, i)]).wait()
            return carry

        lax.fori_loop(0, relayed_rows, settle, 0)

    @pl.when(is_main)
    def _():
        def settle(p, carry):
            @pl.when(field(by_main, p, 1) == 1)
            def _():
                forward_copy(p, outer).wait_send()

            return carry

        lax.fori_loop(0, rows, settle, 0)
        pltpu.make_async_copy(mbuf, mbuf, m_send).wait()
        part = cbuf.at[0, :, pl.ds(0, n_row - 1)]
        pltpu.make_async_copy(part, part, c_send).wait()

    @pl.when(is_side)
    def _():
        part = cbuf.at[:, :, pl.ds(0, n_row - 1)]
        pltpu.make_async_copy(part, part, c_send).wait()
        part = cbuf.at[0, :, 0]
        pltpu.make_async_copy(part, part, c_send).wait()


def side_col(column, depth):
    return lax.rem(column + 2 * depth + 3, 4)


def pack_bytes(members):
    padded = list(members) + [0] * (32 - len(members))
    return [sum(padded[4 * w + i] << (8 * i) for i in range(4)) for w in range(8)]


def on_device(
    a_blocks, a_columns, a_live, atom_rows, b_blocks, b_columns, b_live, c_columns, c_live
):
    n_row, n_col, n_depth = (lax.axis_size(name) for name in ("row", "col", "depth"))
    row, depth = (lax.axis_index(name) for name in ("row", "depth"))
    _, group_count, slots = a_columns.shape
    edge = a_blocks.shape[-1]
    stripe, _, list_width = b_columns.shape
    run, _, targets = c_columns.shape
    stripes = n_row * n_depth
    total = stripe * stripes
    share = targets // n_depth
    width = group_count * slots // stripes
    row_count = n_row * run
    kinds = stripe_kinds(total, stripe, total // n_col)
    senders = {rel // 2 * 2 if rel ^ 1 in kinds and n_depth == 2 else rel for rel in kinds}
    block_count = stripe * list_width
    lanes = -(-width * targets // 128) * 128
    spare = lanes - width * targets

    firsts = jnp.arange(stripes, dtype=jnp.int32)[:, None] * stripe
    a_keys = jnp.where(a_live > 0, a_columns, -total).reshape(stripes, width) - firsts
    a_keys = jnp.repeat(a_keys, targets, axis=1)
    a_keys = jnp.pad(a_keys, ((0, 0), (0, spare)), constant_values=-1)[:, None]
    place = jnp.broadcast_to((atom_rows - row * run).reshape(1, 1, 1), (stripes, 1, lanes))
    table = jnp.tile(c_columns[:, 0, :], (1, width))
    table = jnp.pad(table, ((0, 0), (0, spare)), constant_values=-2)
    pack = jnp.concatenate(
        [
            a_keys,
            place,
            jnp.zeros((stripes, 6, lanes), jnp.int32),
            jnp.broadcast_to(table[None], (stripes, run, lanes)),
        ],
        axis=1,
    )
    b_keys = jnp.where(b_live > 0, b_columns, -1).reshape(-1)
    b_rows = jnp.arange(block_count, dtype=jnp.int32) // list_width
    keys = jnp.broadcast_to(jnp.stack([b_keys, b_rows])[:, :, None], (2, block_count, lanes))
    keep = lax.dynamic_slice_in_dim(c_live[:, 0, :], depth * share, share, 1).reshape(-1)

    operands = (pack, keys, keep, a_blocks.reshape(-1, edge, edge), b_blocks.reshape(-1, edge, edge))
    lists = [
        pltpu.VMEM((row_count, 8 + run, lanes), jnp.int32),
        pltpu.VMEM((row_count + run, lanes), jnp.int32),
        pltpu.SMEM((row_count + run, lanes), jnp.int32),
        pltpu.VMEM((row_count, width, edge, edge), jnp.bfloat16),
        pltpu.VMEM((block_count + 1, edge, edge), jnp.bfloat16),
    ]
    if (n_row, n_col, n_depth) == (4, 4, 2) and sorted(kinds) == [0, 1, 2, 7]:
        body = functools.partial(torus_kernel, slots, kinds)
        scratch = lists + [
            pltpu.VMEM((n_depth, run, n_row, share, edge, edge), jnp.bfloat16),
            pltpu.VMEM((run, n_row, share, edge, edge), jnp.bfloat16),
            pltpu.VMEM((3, run, share, edge, edge), jnp.bfloat16),
            pltpu.SemaphoreType.DMA,
            pltpu.SemaphoreType.DMA,
            pltpu.SemaphoreType.DMA,
            pltpu.SemaphoreType.DMA,
            pltpu.SemaphoreType.DMA((3 * n_col * n_depth,)),
            pltpu.SemaphoreType.DMA((row_count,)),
            pltpu.SemaphoreType.DMA((row_count,)),
            pltpu.SemaphoreType.DMA,
            pltpu.SemaphoreType.DMA((run,)),
            pltpu.SemaphoreType.DMA,
            pltpu.SemaphoreType.DMA((3,)),
        ]
    else:
        body = functools.partial(kernel, n_row, n_col, n_depth, kinds, slots)
        scratch = lists + [
            pltpu.VMEM((n_row, n_depth, run, share, edge, edge), jnp.bfloat16),
            pltpu.VMEM((2, run, share, edge, edge), jnp.bfloat16),
            pltpu.VMEM((len(senders), run, share, edge, edge), jnp.bfloat16),
            pltpu.SemaphoreType.DMA,
            pltpu.SemaphoreType.DMA,
            pltpu.SemaphoreType.DMA,
            pltpu.SemaphoreType.DMA,
            pltpu.SemaphoreType.DMA((n_col * len(kinds),)),
            pltpu.SemaphoreType.DMA((row_count,)),
            pltpu.SemaphoreType.DMA((2,)),
            pltpu.SemaphoreType.DMA((2,)),
            pltpu.SemaphoreType.REGULAR,
            pltpu.SemaphoreType.DMA((n_row, n_depth)),
            pltpu.SemaphoreType.DMA((len(senders),)),
        ]
    result = pl.pallas_call(
        body,
        out_shape=jax.ShapeDtypeStruct((run, share, edge, edge), jnp.bfloat16),
        in_specs=[
            pl.BlockSpec(memory_space=pltpu.VMEM),
            pl.BlockSpec(memory_space=pltpu.VMEM),
            pl.BlockSpec(memory_space=pltpu.SMEM),
            pl.BlockSpec(memory_space=pl.ANY),
            pl.BlockSpec(memory_space=pl.ANY),
        ],
        out_specs=pl.BlockSpec(memory_space=pltpu.VMEM),
        scratch_shapes=scratch,
        compiler_params=pltpu.CompilerParams(
            has_side_effects=True, vmem_limit_bytes=60 * 1024 * 1024
        ),
    )(*operands)
    return result[:, None]


def solution(mesh):
    placed = (
        P(("row", "col", "depth"), None, None, None, None),
        P(("row", "col", "depth"), None, None),
        P(("row", "col", "depth"), None, None),
        P(("row", "col", "depth")),
        P(("row", "depth"), "col", None, None, None),
        P(("row", "depth"), "col", None),
        P(("row", "depth"), "col", None),
        P("row", "col", None),
        P("row", "col", None),
    )
    return jax.shard_map(
        on_device,
        mesh=mesh,
        in_specs=placed,
        out_specs=P("row", "col", "depth", None, None),
        check_vma=False,
    )
```

```python
import functools

import jax
import jax.numpy as jnp
from jax import lax
from jax.experimental import pallas as pl
from jax.experimental.pallas import tpu as pltpu
from jax.sharding import PartitionSpec as P

GW = 10
REACH = 16
MESH = pl.DeviceIdType.MESH


def stripe_kinds(total, stripe, panel):
    kinds = {}
    for rel in range(total // stripe):
        groups = []
        for g in range(stripe // GW):
            first = rel * stripe + g * GW
            if any((k + REACH) % total < panel + 2 * REACH for k in range(first, first + GW)):
                groups.append(g)
        if groups:
            kinds[rel] = (groups[0], groups[-1] + 1)
    return kinds


def flip(index, step, count):
    return lax.rem(index // 2 + step // 2, count // 2) * 2 + lax.rem(index + step, 2)


def kernel(
    n_row, n_col, n_depth, kinds, slots,
    pack_ref, keys_ref, keep_ref, a_ref, b_ref, out_ref,
    lbuf, picks, pick_s, abuf, bbuf, cbuf, mbuf, pbuf,
    l_send, l_recv, s_sem, b_sem, a_send, a_recv, m_send, m_recv, m_free, c_send, c_recv,
):
    row, col, depth = (lax.axis_index(name) for name in ("row", "col", "depth"))
    stripes = n_row * n_depth
    per_panel = stripes // n_col
    run = n_col * n_depth
    rows = n_row * run
    me = (row * n_col + col) * n_depth + depth
    my_stripe = row * n_depth + depth
    my_rel = lax.rem(my_stripe - per_panel * col + stripes, stripes)
    rels = sorted(kinds)
    blocks = b_ref.shape[0]
    share = pbuf.shape[2]
    targets = share * n_depth
    width = a_ref.shape[0] // stripes
    groups = width // slots
    active = functools.reduce(jnp.logical_or, [my_rel == rel for rel in rels])
    paired = [rel for rel in rels if rel ^ 1 in kinds and n_depth == 2]
    lone = [rel for rel in rels if rel not in paired]
    senders = sorted({rel // 2 * 2 if rel in paired else rel for rel in rels})

    def sender(rel):
        return senders.index(rel // 2 * 2 if rel in paired else rel)

    def a_part(ref, rel):
        low, high = kinds[rel]
        return ref.at[pl.ds(low * slots, (high - low) * slots)]

    def list_copy(offset):
        dest = lax.rem(me + offset, rows)
        dest_row, dest_col, dest_depth = dest // run, dest // n_depth % n_col, dest % n_depth
        return pltpu.make_async_remote_copy(
            src_ref=pack_ref.at[dest_row * n_depth + dest_depth],
            dst_ref=lbuf.at[me],
            send_sem=l_send,
            recv_sem=l_recv,
            device_id=(dest_row, dest_col, dest_depth),
            device_id_type=MESH,
        )

    pltpu.make_async_copy(pack_ref.at[my_stripe], lbuf.at[me], l_recv).start()

    def send_list(offset, carry):
        list_copy(offset).start()
        return carry

    lax.fori_loop(1, rows, send_list, 0)

    b_copy = pltpu.make_async_copy(b_ref, bbuf.at[pl.ds(0, blocks)], b_sem)

    @pl.when(active)
    def _():
        b_copy.start()

    sends = []
    for t in reversed(range(n_col)):
        c = flip(row, t, n_col)
        for rel in rels:
            s = lax.rem(per_panel * c + rel, stripes)
            low, high = kinds[rel]
            src = a_ref.at[pl.ds(s * width + low * slots, (high - low) * slots)]
            mine = (my_stripe == s) & (col == c)
            remote = pltpu.make_async_remote_copy(
                src_ref=src,
                dst_ref=a_part(abuf.at[me], rel),
                send_sem=a_send.at[len(sends)],
                recv_sem=a_recv.at[me],
                device_id=(s // n_depth, c, s % n_depth),
                device_id_type=MESH,
            )
            local = pltpu.make_async_copy(src, a_part(abuf.at[me], rel), a_recv.at[me])
            sends.append((mine, remote))

            @pl.when(mine)
            def _(local=local):
                local.start()

            @pl.when(jnp.logical_not(mine))
            def _(remote=remote):
                remote.start()

    for rel in rels:
        low, high = kinds[rel]
        gaps = [g for g in range(groups) if not low <= g < high]
        if gaps:

            @pl.when(my_rel == rel)
            def _(gaps=gaps):
                def clear(p, carry):
                    for g in gaps:
                        for v in range(g * slots, (g + 1) * slots):
                            abuf[p, v] = jnp.zeros(abuf.shape[2:], abuf.dtype)
                    return carry

                lax.fori_loop(0, rows, clear, 0)

    pltpu.make_async_copy(lbuf, lbuf, l_recv).wait()
    lanes = lbuf.shape[2]

    def match(p, carry):
        column_row = lbuf[p, 0:1, :]
        place = lbuf[p, 1:2, :]
        table = lbuf[(p // run * n_col + col) * n_depth, 8:, :]
        at = lax.broadcasted_iota(jnp.int32, (run, lanes), 0)
        wanted = jnp.sum(jnp.where(at == place, table, 0), axis=0, keepdims=True)
        hit = (keys_ref[1] == column_row) & (keys_ref[0] == wanted)
        number = lax.broadcasted_iota(jnp.int32, (blocks, lanes), 0)
        picks[pl.ds(p, 1), :] = jnp.min(
            jnp.where(hit, number, blocks), axis=0, keepdims=True
        )
        return carry

    lax.fori_loop(0, rows, match, 0)
    for q in range(run):
        picks[pl.ds(rows + q, 1), :] = lbuf[row * run + q, 1:2, :]
    to_scalars = pltpu.make_async_copy(picks, pick_s, s_sem)
    to_scalars.start()
    to_scalars.wait()

    def share_copy(target_row, d, slot):
        return pltpu.make_async_remote_copy(
            src_ref=cbuf.at[target_row, d],
            dst_ref=pbuf.at[slot],
            send_sem=c_send.at[target_row, d],
            recv_sem=c_recv.at[slot],
            device_id=(target_row, col, d),
            device_id_type=MESH,
        )

    def start_share(target_row, d, slot):
        own = (target_row == row) & (depth == d)

        @pl.when(jnp.logical_not(own))
        def _():
            share_copy(target_row, d, slot).start()

        @pl.when(own)
        def _():
            pltpu.make_async_copy(cbuf.at[target_row, d], pbuf.at[slot], c_recv.at[slot]).start()

    def settle_share(target_row, d):
        @pl.when(jnp.logical_not((target_row == row) & (depth == d)))
        def _():
            share_copy(target_row, d, 0).wait_send()

    is_paired = functools.reduce(jnp.logical_or, [my_rel == rel for rel in paired], False)

    def mate_copy(t, target_row):
        return pltpu.make_async_remote_copy(
            src_ref=cbuf.at[target_row, 1 - depth],
            dst_ref=mbuf.at[t % 2],
            send_sem=m_send.at[t % 2],
            recv_sem=m_recv.at[t % 2],
            device_id=(row, col, 1 - depth),
            device_id_type=MESH,
        )

    @pl.when(active)
    def _():
        b_copy.wait()
        bbuf[blocks] = jnp.zeros(bbuf.shape[1:], bbuf.dtype)

        def one_run(t, carry):
            target_row = flip(col, n_row - 1 - t, n_row)

            def one_row(q, inner):
                p = target_row * run + q
                for rel in rels:

                    @pl.when(my_rel == rel)
                    def _(rel=rel):
                        part = a_part(abuf.at[p], rel)
                        pltpu.make_async_copy(part, part, a_recv.at[p]).wait()

                for u in range(0, targets, 2):
                    total = None
                    for v in range(0, width, 2):
                        left = jnp.concatenate([abuf[p, v], abuf[p, v + 1]], axis=1)
                        right = jnp.concatenate(
                            [
                                jnp.concatenate(
                                    [
                                        bbuf[pick_s[p, (v + i) * targets + u]],
                                        bbuf[pick_s[p, (v + i) * targets + u + 1]],
                                    ],
                                    axis=1,
                                )
                                for i in range(2)
                            ],
                            axis=0,
                        )
                        term = jnp.dot(left, right, preferred_element_type=jnp.float32)
                        total = term if total is None else total + term
                    edge = abuf.shape[-1]
                    for i in range(2):
                        cbuf[target_row, (u + i) // share, q, (u + i) % share] = total[
                            :, i * edge : (i + 1) * edge
                        ].astype(cbuf.dtype)
                return inner

            lax.fori_loop(0, run, one_row, 0)
            for rel in lone:

                @pl.when(my_rel == rel)
                def _(rel=rel):
                    for d in range(n_depth):
                        start_share(target_row, d, sender(rel))

            if paired:

                @pl.when(is_paired)
                def _():
                    @pl.when(t >= 2)
                    def _():
                        pl.semaphore_wait(m_free, 1)

                    exchange = mate_copy(t, target_row)
                    exchange.start()
                    exchange.wait()

                    def merge(q, inner):
                        for u in range(share):
                            cbuf[target_row, depth, q, u] = (
                                cbuf[target_row, depth, q, u].astype(jnp.float32)
                                + mbuf[t % 2, q, u].astype(jnp.float32)
                            ).astype(cbuf.dtype)
                        return inner

                    lax.fori_loop(0, run, merge, 0)

                    @pl.when(t < n_row - 2)
                    def _():
                        pl.semaphore_signal(
                            m_free,
                            inc=1,
                            device_id=(row, col, 1 - depth),
                            device_id_type=MESH,
                        )

                for slot, first in enumerate(senders):
                    if first in paired:

                        @pl.when(my_rel // 2 * 2 == first)
                        def _(slot=slot):
                            start_share(target_row, depth, slot)

            return carry

        lax.fori_loop(0, n_row, one_run, 0)

    for slot in range(len(senders)):
        pltpu.make_async_copy(pbuf.at[slot], pbuf.at[slot], c_recv.at[slot]).wait()

    def finish(i, carry):
        q = jnp.int32(0)
        for j in range(run):
            q = jnp.where(pick_s[rows + j, 0] == i, j, q)
        for u in range(share):
            value = pbuf[0, q, u].astype(jnp.float32)
            for slot in range(1, len(senders)):
                value = value + pbuf[slot, q, u].astype(jnp.float32)
            kept = keep_ref[i * share + u] > 0
            out_ref[i, u] = jnp.where(kept, value, jnp.float32(0.0)).astype(out_ref.dtype)
        return carry

    lax.fori_loop(0, run, finish, 0)

    sent = lbuf.at[pl.ds(0, rows - 1)]
    pltpu.make_async_copy(sent, sent, l_send).wait()
    for mine, remote in sends:
        @pl.when(jnp.logical_not(mine))
        def _(remote=remote):
            remote.wait_send()

    def settle(target_row, carry):
        for rel in lone:

            @pl.when(my_rel == rel)
            def _():
                for d in range(n_depth):
                    settle_share(target_row, d)

        if paired:

            @pl.when(is_paired)
            def _():
                settle_share(target_row, depth)

        return carry

    lax.fori_loop(0, n_row, settle, 0)


BATCH = 4
BY_MAIN_FIRST, VIA_RELAY, DIRECT = 0, 1, 2
ORDER = (
    (
        0xb1fd85a9, 0x7e10a5bc, 0x9afe862c, 0x4827ce31, 0x2db194f7, 0x5168ae40, 0xb42f8c70, 0xd4032c59,
        0x3ca02b1e, 0xc7bfae45, 0xba286c3, 0xd59e3c16, 0x8263a749, 0x9cea405f, 0x1b0a3e26, 0x18c6afe4,
        0xf628410a, 0xf5e4d0c8, 0x7204aeb1, 0x6c8d49a7, 0x3b70d2f8, 0xe54c682d, 0x295140ab, 0xd24ec5f0,
        0x3aedc2b7, 0x5ac1629e, 0xbf8640ae, 0xc35f7a19, 0xa6c920df, 0x741068c2, 0x90fe4b52, 0x5f136b47,
    ),
    (
        0xc460723e, 0x863f249d, 0x43b7d501, 0xbdf59a60, 0x3c6ae85, 0x93fbd7c2, 0x16a3de59, 0x7e6b8af1,
        0x748d5f96, 0x12d39860, 0x7d95e14f, 0xf0a2b784, 0x51f0cedb, 0x12d83b67, 0xd7845fc9, 0xb027d953,
        0x5ec937bd, 0x396ab127, 0xfc36d589, 0xbf1e2035, 0x1e4c596a, 0x937b0fa1, 0xfc3d768e, 0x9a63b178,
        0x9085641f, 0xf84d30b7, 0x7d15392c, 0xed28406b, 0x531b748e, 0xad593bef, 0x68d1ca73, 0x2a8e9cd0,
    ),
)
ROUTES = (
    0x56a0, 0x55a0, 0x5526, 0x568a, 0x144a, 0xa559, 0x65a2, 0x4489,
    0x65a0, 0xa518, 0x590a, 0x5608, 0x1642, 0x258a, 0x6682, 0x6652,
    0x8599, 0x8299, 0xa258, 0x8194, 0x2095, 0xa065, 0x245a, 0xa59,
    0x6211, 0x8a59, 0x655a, 0xa114, 0xa295, 0x9855, 0xa55, 0xa95,
)
BY_MAIN = (
    0x80c0b03, 0x100d143, 0x7c98, 0x9000e04, 0x20700090, 0x193e0000, 0xc28b0080, 0xc0d03010,
)
RELAYED = (
    (7, 16, 5, 28, 30, 31, 29, 17, 23, 20, 21, 25, 24),
    (2, 30, 27, 19, 20, 21, 29, 31, 28),
    (9, 31, 18, 19, 16, 17, 15, 30, 26, 24, 25, 23, 29, 28, 20, 5, 27, 22),
    (12, 21, 4, 5, 25, 29, 15, 22, 26, 23, 30, 18),
    (19, 10, 26, 27, 6, 2, 16, 9, 5, 8, 1, 13),
    (22, 0, 12, 13, 14, 15, 1, 16, 5, 6, 7, 8, 2, 3, 11, 26, 4, 9),
    (29, 1, 4, 12, 10, 11, 2, 0, 3),
    (24, 15, 26, 3, 0, 1, 2, 8, 14, 10, 11, 6, 7),
)
MAIN_ROWS = (
    (0, 1, 14, 3, 11, 2, 10, 27, 8, 22, 19, 9, 15, 26, 18, 7, 6, 30, 12, 13, 23, 20, 21, 25, 24, 29, 4, 31, 5, 28, 16, 17),
    (10, 11, 2, 1, 3, 13, 0, 8, 9, 14, 31, 6, 7, 16, 17, 24, 12, 19, 21, 4, 20, 25, 29, 28, 15, 22, 23, 30, 18, 5, 26, 27),
    (20, 21, 18, 28, 29, 30, 31, 23, 22, 17, 0, 25, 24, 14, 15, 12, 7, 19, 27, 10, 11, 2, 6, 3, 9, 16, 8, 1, 13, 5, 4, 26),
    (30, 31, 17, 28, 29, 20, 21, 4, 9, 22, 23, 12, 5, 16, 13, 24, 25, 1, 19, 18, 10, 8, 6, 11, 7, 2, 0, 3, 27, 26, 14, 15),
)
SIDE_ROWS = (
    (6, 7, 14, 15, 16, 5, 28, 2, 30, 31, 22, 29, 17, 23, 26, 20, 21, 12, 13, 4, 25, 24, 0, 1, 11, 10, 8, 3, 9, 19, 18, 27),
    (3, 2, 11, 30, 10, 23, 26, 18, 27, 7, 19, 20, 21, 16, 29, 4, 17, 22, 31, 0, 1, 28, 14, 8, 13, 9, 15, 12, 6, 25, 24, 5),
    (8, 9, 31, 18, 19, 0, 1, 16, 17, 22, 15, 30, 26, 24, 25, 6, 23, 5, 29, 2, 27, 10, 11, 3, 13, 14, 28, 7, 20, 12, 21, 4),
    (13, 12, 21, 14, 20, 4, 5, 28, 25, 29, 31, 15, 8, 19, 22, 16, 26, 23, 1, 7, 30, 6, 17, 18, 3, 10, 11, 2, 0, 9, 24, 27),
    (18, 19, 10, 11, 17, 26, 27, 3, 6, 2, 0, 16, 23, 12, 9, 15, 5, 8, 30, 24, 1, 25, 14, 13, 28, 20, 21, 29, 31, 22, 7, 4),
    (23, 22, 0, 12, 13, 30, 31, 14, 15, 9, 1, 16, 5, 6, 7, 25, 8, 26, 2, 29, 4, 20, 21, 18, 28, 17, 3, 24, 11, 19, 10, 27),
    (28, 29, 20, 1, 21, 5, 8, 13, 4, 24, 12, 10, 11, 15, 2, 27, 14, 9, 0, 30, 31, 3, 17, 22, 18, 23, 16, 19, 25, 6, 7, 26),
    (25, 24, 16, 17, 15, 26, 3, 29, 0, 1, 9, 2, 8, 14, 5, 10, 11, 18, 19, 27, 6, 7, 30, 31, 20, 21, 22, 28, 23, 12, 13, 4),
)


def pick_word(words, index):
    value = jnp.int32(0)
    for i, word in enumerate(words):
        word = jnp.int32(word - (1 << 32) if word >> 31 else word)
        value = jnp.where(index == i, word, value)
    return value


def field(word, index, bits):
    return lax.shift_right_logical(word, index * bits) & ((1 << bits) - 1)


def torus_kernel(
    slots, held,
    pack_ref, keys_ref, keep_ref, a_ref, b_ref, out_ref,
    lbuf, picks, pick_s, abuf, bbuf, cbuf, mbuf, pbuf,
    l_send, l_recv, s_sem, b_sem, a_send, a_recv, f_send,
    m_send, m_recv, c_send, c_recv,
):
    n_row, n_col, n_depth = 4, 4, 2
    row, col, depth = (lax.axis_index(name) for name in ("row", "col", "depth"))
    run = n_col * n_depth
    rows = n_row * run
    me = (row * n_col + col) * n_depth + depth
    my_stripe = row * n_depth + depth
    blocks = b_ref.shape[0]
    share = pbuf.shape[2]
    targets = share * n_depth
    width = abuf.shape[1]
    half = width // 2
    edge = abuf.shape[-1]
    outer = side_col(row, depth)
    is_main = col == row
    is_side = col == outer
    is_relay = col == side_col(row, 1 - depth)
    active = is_main | is_side
    my_edge = depth * half

    def list_copy(offset):
        dest = lax.rem(me + offset, rows)
        dest_row, dest_col, dest_depth = dest // run, dest // n_depth % n_col, dest % n_depth
        return pltpu.make_async_remote_copy(
            src_ref=pack_ref.at[dest_row * n_depth + dest_depth],
            dst_ref=lbuf.at[me],
            send_sem=l_send,
            recv_sem=l_recv,
            device_id=(dest_row, dest_col, dest_depth),
            device_id_type=MESH,
        )

    pltpu.make_async_copy(pack_ref.at[my_stripe], lbuf.at[me], l_recv).start()

    def send_list(offset, carry):
        list_copy(offset).start()
        return carry

    lax.fori_loop(1, rows, send_list, 0)

    b_copy = pltpu.make_async_copy(b_ref, bbuf.at[pl.ds(0, blocks)], b_sem)

    @pl.when(active)
    def _():
        b_copy.start()

    sends = []

    def send_part(wanted, src, low, place):
        mine = (row == place[0]) & (col == place[1]) & (depth == place[2])
        dst = abuf.at[me, pl.ds(low, half)]
        remote = pltpu.make_async_remote_copy(
            src_ref=src,
            dst_ref=dst,
            send_sem=a_send.at[len(sends)],
            recv_sem=a_recv.at[me],
            device_id=place,
            device_id_type=MESH,
        )
        local = pltpu.make_async_copy(src, dst, a_recv.at[me])
        away = wanted & jnp.logical_not(mine)
        sends.append((away, remote))

        @pl.when(wanted & mine)
        def _():
            local.start()

        @pl.when(away)
        def _():
            remote.start()

    my_order = [pick_word(words, me) for words in ORDER]
    my_routes = pick_word(ROUTES, me)
    for t in range(2 * n_col * n_depth):
        entry = field(my_order[t // 8], t % 8, 4)
        s, is_mid = entry // 2, entry % 2 == 1
        c, d = s // n_depth, s % n_depth
        route = field(my_routes, s, 2)
        side = side_col(c, d)
        low = jnp.where(is_mid, half - d * half, d * half)
        src = a_ref.at[pl.ds(s * width + low, half)]
        via = (route == VIA_RELAY) & jnp.logical_not(is_mid)
        place = (c, jnp.where(via, side, c), jnp.where(via, 1 - d, d))
        send_part(me >= 0, src, low, place)
        twice = (route == DIRECT) & jnp.logical_not(is_mid)
        send_part(twice, src, low, (c, side, d))

    far_edge = (1 - depth) * half

    def relay_copy(p, dest_col):
        part = abuf.at[p, pl.ds(far_edge, half)]
        return pltpu.make_async_remote_copy(
            src_ref=part,
            dst_ref=part,
            send_sem=f_send.at[p],
            recv_sem=a_recv.at[p],
            device_id=(row, dest_col, 1 - depth),
            device_id_type=MESH,
        )

    def wait_blocks(p, count):
        part = abuf.at[p, pl.ds(0, count)]
        pltpu.make_async_copy(part, part, a_recv.at[p]).wait()

    other_stripe = row * n_depth + 1 - depth
    relayed_rows = pick_word([len(r) for r in RELAYED], other_stripe)
    relay_words = [
        pick_word([pack_bytes(r)[w] for r in RELAYED], other_stripe) for w in range(rows // 4)
    ]

    def table_row(words, i):
        word = words[0]
        for w in range(1, len(words)):
            word = jnp.where(i // 4 == w, words[w], word)
        return field(word, i % 4, 8)

    @pl.when(is_relay)
    def _():
        def relay(i, carry):
            p = table_row(relay_words, i)
            wait_blocks(p, half)
            relay_copy(p, row).start()
            relay_copy(p, col).start()
            return carry

        lax.fori_loop(0, relayed_rows, relay, 0)

    pltpu.make_async_copy(lbuf, lbuf, l_recv).wait()
    lanes = lbuf.shape[2]

    def match(p, carry):
        column_row = lbuf[p, 0:1, :]
        place = lbuf[p, 1:2, :]
        table = lbuf[(p // run * n_col + col) * n_depth, 8:, :]
        at = lax.broadcasted_iota(jnp.int32, (run, lanes), 0)
        wanted = jnp.sum(jnp.where(at == place, table, 0), axis=0, keepdims=True)
        hit = (keys_ref[1] == column_row) & (keys_ref[0] == wanted)
        number = lax.broadcasted_iota(jnp.int32, (blocks, lanes), 0)
        picks[pl.ds(p, 1), :] = jnp.min(
            jnp.where(hit, number, blocks), axis=0, keepdims=True
        )
        return carry

    lax.fori_loop(0, rows, match, 0)
    for q in range(run):
        picks[pl.ds(rows + q, 1), :] = lbuf[row * run + q, 1:2, :]
    to_scalars = pltpu.make_async_copy(picks, pick_s, s_sem)
    to_scalars.start()
    to_scalars.wait()

    main_words = [pick_word([pack_bytes(r)[w] for r in MAIN_ROWS], row) for w in range(run)]
    side_words = [pick_word([pack_bytes(r)[w] for r in SIDE_ROWS], my_stripe) for w in range(run)]
    by_main = pick_word(BY_MAIN, my_stripe)

    def forward_copy(p, dest_col):
        part = abuf.at[p, pl.ds(my_edge, half)]
        return pltpu.make_async_remote_copy(
            src_ref=part,
            dst_ref=part,
            send_sem=f_send.at[p],
            recv_sem=a_recv.at[p],
            device_id=(row, dest_col, depth),
            device_id_type=MESH,
        )

    def batch_rows(words, b):
        return [table_row(words, b * BATCH + i) for i in range(BATCH)]

    def multiply(p, b, at, base, count):
        left = jnp.concatenate([abuf[p, base + v] for v in range(count)], axis=1)
        for u in range(0, targets, 2):
            right = jnp.concatenate(
                [
                    jnp.concatenate(
                        [
                            bbuf[pick_s[p, (base + v) * targets + u]],
                            bbuf[pick_s[p, (base + v) * targets + u + 1]],
                        ],
                        axis=1,
                    )
                    for v in range(count)
                ],
                axis=0,
            )
            total = jnp.dot(left, right, preferred_element_type=jnp.float32)
            for i in range(2):
                cbuf[(u + i) // share, b, at, (u + i) % share] = total[
                    :, i * edge : (i + 1) * edge
                ].astype(cbuf.dtype)

    def start_share(p, b, at, d, slot):
        target, q = p // run, p % run
        own = (row == target) & (depth == d)
        src = cbuf.at[d, b, at]
        dst = pbuf.at[slot, q]

        @pl.when(jnp.logical_not(own))
        def _():
            pltpu.make_async_remote_copy(
                src_ref=src,
                dst_ref=dst,
                send_sem=c_send,
                recv_sem=c_recv.at[slot],
                device_id=(target, col, d),
                device_id_type=MESH,
            ).start()

        @pl.when(own)
        def _():
            pltpu.make_async_copy(src, dst, c_recv.at[slot]).start()

    def mate_copy(b):
        return pltpu.make_async_remote_copy(
            src_ref=cbuf.at[1 - depth, b],
            dst_ref=mbuf.at[b],
            send_sem=m_send,
            recv_sem=m_recv.at[b],
            device_id=(row, col, 1 - depth),
            device_id_type=MESH,
        )

    @pl.when(active)
    def _():
        b_copy.wait()
        bbuf[blocks] = jnp.zeros(bbuf.shape[1:], bbuf.dtype)

    @pl.when(is_main)
    def _():
        def one_batch(b, carry):
            @pl.when(b < rows // BATCH)
            def _():
                members = batch_rows(main_words, b)
                for p in members:

                    @pl.when(field(by_main, p, 1) == 1)
                    def _(p=p):
                        wait_blocks(p, width)
                        forward_copy(p, outer).start()

                for p in members:

                    @pl.when(field(by_main, p, 1) == 0)
                    def _(p=p):
                        wait_blocks(p, width)

                def one_row(i, inner):
                    multiply(table_row(main_words, b * BATCH + i), b, i, 0, width)
                    return inner

                lax.fori_loop(0, BATCH, one_row, 0)
                mate_copy(b).start()

            @pl.when(b > 0)
            def _():
                last = b - 1
                pltpu.make_async_copy(mbuf.at[last], mbuf.at[last], m_recv.at[last]).wait()

                def merge(i, inner):
                    for u in range(share):
                        cbuf[depth, last, i, u] = (
                            cbuf[depth, last, i, u].astype(jnp.float32)
                            + mbuf[last, i, u].astype(jnp.float32)
                        ).astype(cbuf.dtype)
                    return inner

                lax.fori_loop(0, BATCH, merge, 0)
                for i, p in enumerate(batch_rows(main_words, last)):
                    start_share(p, last, i, depth, 0)

            return carry

        lax.fori_loop(0, rows // BATCH + 1, one_batch, 0)

    @pl.when(is_side)
    def _():
        def one_batch(b, carry):
            members = batch_rows(side_words, b)
            for p in members:
                wait_blocks(p, half)

            def one_row(i, inner):
                multiply(table_row(side_words, b * BATCH + i), b, i, my_edge, half)
                return inner

            lax.fori_loop(0, BATCH, one_row, 0)
            for i, p in enumerate(members):
                for d in range(n_depth):
                    start_share(p, b, i, d, 1 + depth)
            return carry

        lax.fori_loop(0, rows // BATCH, one_batch, 0)

    for slot in range(pbuf.shape[0]):
        pltpu.make_async_copy(pbuf.at[slot], pbuf.at[slot], c_recv.at[slot]).wait()

    def finish(i, carry):
        q = jnp.int32(0)
        for j in range(run):
            q = jnp.where(pick_s[rows + j, 0] == i, j, q)
        for u in range(share):
            value = pbuf[0, q, u].astype(jnp.float32)
            for slot in range(1, pbuf.shape[0]):
                value = value + pbuf[slot, q, u].astype(jnp.float32)
            out_ref[i, u] = value.astype(out_ref.dtype)
        return carry

    lax.fori_loop(0, run, finish, 0)

    sent = lbuf.at[pl.ds(0, rows - 1)]
    pltpu.make_async_copy(sent, sent, l_send).wait()
    for away, remote in sends:

        @pl.when(away)
        def _(remote=remote):
            remote.wait_send()

    @pl.when(is_relay)
    def _():
        def settle(i, carry):
            part = abuf.at[0]
            pltpu.make_async_copy(part, part, f_send.at[table_row(relay_words, i)]).wait()
            return carry

        lax.fori_loop(0, relayed_rows, settle, 0)

    @pl.when(is_main)
    def _():
        def settle(p, carry):
            @pl.when(field(by_main, p, 1) == 1)
            def _():
                forward_copy(p, outer).wait_send()

            return carry

        lax.fori_loop(0, rows, settle, 0)
        pltpu.make_async_copy(mbuf, mbuf, m_send).wait()
        part = abuf.at[pl.ds(0, (rows - run) * share // width)]
        pltpu.make_async_copy(part, part, c_send).wait()

    @pl.when(is_side)
    def _():
        part = abuf.at[pl.ds(0, (2 * rows - run) * share // width)]
        pltpu.make_async_copy(part, part, c_send).wait()


def side_col(column, depth):
    return lax.rem(column + 2 * depth + 3, 4)


def pack_bytes(members):
    padded = list(members) + [0] * (32 - len(members))
    return [sum(padded[4 * w + i] << (8 * i) for i in range(4)) for w in range(8)]


def on_device(
    a_blocks, a_columns, a_live, atom_rows, b_blocks, b_columns, b_live, c_columns, c_live
):
    n_row, n_col, n_depth = (lax.axis_size(name) for name in ("row", "col", "depth"))
    row, depth = (lax.axis_index(name) for name in ("row", "depth"))
    _, group_count, slots = a_columns.shape
    edge = a_blocks.shape[-1]
    stripe, _, list_width = b_columns.shape
    run, _, targets = c_columns.shape
    stripes = n_row * n_depth
    total = stripe * stripes
    share = targets // n_depth
    width = group_count * slots // stripes
    row_count = n_row * run
    kinds = stripe_kinds(total, stripe, total // n_col)
    senders = {rel // 2 * 2 if rel ^ 1 in kinds and n_depth == 2 else rel for rel in kinds}
    block_count = stripe * list_width
    lanes = -(-width * targets // 128) * 128
    spare = lanes - width * targets

    firsts = jnp.arange(stripes, dtype=jnp.int32)[:, None] * stripe
    a_keys = jnp.where(a_live > 0, a_columns, -total).reshape(stripes, width) - firsts
    a_keys = jnp.repeat(a_keys, targets, axis=1)
    a_keys = jnp.pad(a_keys, ((0, 0), (0, spare)), constant_values=-1)[:, None]
    place = jnp.broadcast_to((atom_rows - row * run).reshape(1, 1, 1), (stripes, 1, lanes))
    table = jnp.tile(c_columns[:, 0, :], (1, width))
    table = jnp.pad(table, ((0, 0), (0, spare)), constant_values=-2)
    pack = jnp.concatenate(
        [
            a_keys,
            place,
            jnp.zeros((stripes, 6, lanes), jnp.int32),
            jnp.broadcast_to(table[None], (stripes, run, lanes)),
        ],
        axis=1,
    )
    b_keys = jnp.where(b_live > 0, b_columns, -1).reshape(-1)
    b_rows = jnp.arange(block_count, dtype=jnp.int32) // list_width
    keys = jnp.broadcast_to(jnp.stack([b_keys, b_rows])[:, :, None], (2, block_count, lanes))
    keep = lax.dynamic_slice_in_dim(c_live[:, 0, :], depth * share, share, 1).reshape(-1)

    operands = (pack, keys, keep, a_blocks.reshape(-1, edge, edge), b_blocks.reshape(-1, edge, edge))
    lists = [
        pltpu.VMEM((row_count, 8 + run, lanes), jnp.int32),
        pltpu.VMEM((row_count + run, lanes), jnp.int32),
        pltpu.SMEM((row_count + run, lanes), jnp.int32),
        pltpu.VMEM((row_count, width, edge, edge), jnp.bfloat16),
        pltpu.VMEM((block_count + 1, edge, edge), jnp.bfloat16),
    ]
    relayed = (n_row, n_col, n_depth) == (4, 4, 2) and sorted(kinds) == [0, 1, 2, 7]
    if relayed:
        body = functools.partial(torus_kernel, slots, kinds)
        scratch = lists + [
            pltpu.VMEM((n_depth, row_count // BATCH, BATCH, share, edge, edge), jnp.bfloat16),
            pltpu.VMEM((row_count // BATCH, BATCH, share, edge, edge), jnp.bfloat16),
            pltpu.VMEM((3, run, share, edge, edge), jnp.bfloat16),
            pltpu.SemaphoreType.DMA,
            pltpu.SemaphoreType.DMA,
            pltpu.SemaphoreType.DMA,
            pltpu.SemaphoreType.DMA,
            pltpu.SemaphoreType.DMA((4 * n_col * n_depth,)),
            pltpu.SemaphoreType.DMA((row_count,)),
            pltpu.SemaphoreType.DMA((row_count,)),
            pltpu.SemaphoreType.DMA,
            pltpu.SemaphoreType.DMA((row_count // BATCH,)),
            pltpu.SemaphoreType.DMA,
            pltpu.SemaphoreType.DMA((3,)),
        ]
    else:
        body = functools.partial(kernel, n_row, n_col, n_depth, kinds, slots)
        scratch = lists + [
            pltpu.VMEM((n_row, n_depth, run, share, edge, edge), jnp.bfloat16),
            pltpu.VMEM((2, run, share, edge, edge), jnp.bfloat16),
            pltpu.VMEM((len(senders), run, share, edge, edge), jnp.bfloat16),
            pltpu.SemaphoreType.DMA,
            pltpu.SemaphoreType.DMA,
            pltpu.SemaphoreType.DMA,
            pltpu.SemaphoreType.DMA,
            pltpu.SemaphoreType.DMA((n_col * len(kinds),)),
            pltpu.SemaphoreType.DMA((row_count,)),
            pltpu.SemaphoreType.DMA((2,)),
            pltpu.SemaphoreType.DMA((2,)),
            pltpu.SemaphoreType.REGULAR,
            pltpu.SemaphoreType.DMA((n_row, n_depth)),
            pltpu.SemaphoreType.DMA((len(senders),)),
        ]
    result = pl.pallas_call(
        body,
        out_shape=jax.ShapeDtypeStruct((run, share, edge, edge), jnp.bfloat16),
        in_specs=[
            pl.BlockSpec(memory_space=pltpu.VMEM),
            pl.BlockSpec(memory_space=pltpu.VMEM),
            pl.BlockSpec(memory_space=pltpu.SMEM),
            pl.BlockSpec(memory_space=pl.ANY),
            pl.BlockSpec(memory_space=pl.ANY),
        ],
        out_specs=pl.BlockSpec(memory_space=pltpu.VMEM),
        scratch_shapes=scratch,
        compiler_params=pltpu.CompilerParams(
            has_side_effects=True, vmem_limit_bytes=60 * 1024 * 1024
        ),
    )(*operands)
    if relayed:
        wanted = lax.dynamic_slice_in_dim(c_live, depth * share, share, 2) > 0
        return jnp.where(wanted[..., None, None], result[:, None], jnp.bfloat16(0.0))
    return result[:, None]


def solution(mesh):
    placed = (
        P(("row", "col", "depth"), None, None, None, None),
        P(("row", "col", "depth"), None, None),
        P(("row", "col", "depth"), None, None),
        P(("row", "col", "depth")),
        P(("row", "depth"), "col", None, None, None),
        P(("row", "depth"), "col", None),
        P(("row", "depth"), "col", None),
        P("row", "col", None),
        P("row", "col", None),
    )
    return jax.shard_map(
        on_device,
        mesh=mesh,
        in_specs=placed,
        out_specs=P("row", "col", "depth", None, None),
        check_vma=False,
    )
```

```python
import functools

import jax
import jax.numpy as jnp
from jax import lax
from jax.experimental import pallas as pl
from jax.experimental.pallas import tpu as pltpu
from jax.sharding import PartitionSpec as P

GW = 10
REACH = 16
MESH = pl.DeviceIdType.MESH


def stripe_kinds(total, stripe, panel):
    kinds = {}
    for rel in range(total // stripe):
        groups = []
        for g in range(stripe // GW):
            first = rel * stripe + g * GW
            if any((k + REACH) % total < panel + 2 * REACH for k in range(first, first + GW)):
                groups.append(g)
        if groups:
            kinds[rel] = (groups[0], groups[-1] + 1)
    return kinds


def flip(index, step, count):
    return lax.rem(index // 2 + step // 2, count // 2) * 2 + lax.rem(index + step, 2)


def kernel(
    n_row, n_col, n_depth, kinds, slots,
    pack_ref, keys_ref, keep_ref, a_ref, b_ref, out_ref,
    lbuf, picks, pick_s, abuf, bbuf, cbuf, mbuf, pbuf,
    l_send, l_recv, s_sem, b_sem, a_send, a_recv, m_send, m_recv, m_free, c_send, c_recv,
):
    row, col, depth = (lax.axis_index(name) for name in ("row", "col", "depth"))
    stripes = n_row * n_depth
    per_panel = stripes // n_col
    run = n_col * n_depth
    rows = n_row * run
    me = (row * n_col + col) * n_depth + depth
    my_stripe = row * n_depth + depth
    my_rel = lax.rem(my_stripe - per_panel * col + stripes, stripes)
    rels = sorted(kinds)
    blocks = b_ref.shape[0]
    share = pbuf.shape[2]
    targets = share * n_depth
    width = a_ref.shape[0] // stripes
    groups = width // slots
    active = functools.reduce(jnp.logical_or, [my_rel == rel for rel in rels])
    paired = [rel for rel in rels if rel ^ 1 in kinds and n_depth == 2]
    lone = [rel for rel in rels if rel not in paired]
    senders = sorted({rel // 2 * 2 if rel in paired else rel for rel in rels})

    def sender(rel):
        return senders.index(rel // 2 * 2 if rel in paired else rel)

    def a_part(ref, rel):
        low, high = kinds[rel]
        return ref.at[pl.ds(low * slots, (high - low) * slots)]

    def list_copy(offset):
        dest = lax.rem(me + offset, rows)
        dest_row, dest_col, dest_depth = dest // run, dest // n_depth % n_col, dest % n_depth
        return pltpu.make_async_remote_copy(
            src_ref=pack_ref.at[dest_row * n_depth + dest_depth],
            dst_ref=lbuf.at[me],
            send_sem=l_send,
            recv_sem=l_recv,
            device_id=(dest_row, dest_col, dest_depth),
            device_id_type=MESH,
        )

    pltpu.make_async_copy(pack_ref.at[my_stripe], lbuf.at[me], l_recv).start()

    def send_list(offset, carry):
        list_copy(offset).start()
        return carry

    lax.fori_loop(1, rows, send_list, 0)

    b_copy = pltpu.make_async_copy(b_ref, bbuf.at[pl.ds(0, blocks)], b_sem)

    @pl.when(active)
    def _():
        b_copy.start()

    sends = []
    for t in reversed(range(n_col)):
        c = flip(row, t, n_col)
        for rel in rels:
            s = lax.rem(per_panel * c + rel, stripes)
            low, high = kinds[rel]
            src = a_ref.at[pl.ds(s * width + low * slots, (high - low) * slots)]
            mine = (my_stripe == s) & (col == c)
            remote = pltpu.make_async_remote_copy(
                src_ref=src,
                dst_ref=a_part(abuf.at[me], rel),
                send_sem=a_send.at[len(sends)],
                recv_sem=a_recv.at[me],
                device_id=(s // n_depth, c, s % n_depth),
                device_id_type=MESH,
            )
            local = pltpu.make_async_copy(src, a_part(abuf.at[me], rel), a_recv.at[me])
            sends.append((mine, remote))

            @pl.when(mine)
            def _(local=local):
                local.start()

            @pl.when(jnp.logical_not(mine))
            def _(remote=remote):
                remote.start()

    for rel in rels:
        low, high = kinds[rel]
        gaps = [g for g in range(groups) if not low <= g < high]
        if gaps:

            @pl.when(my_rel == rel)
            def _(gaps=gaps):
                def clear(p, carry):
                    for g in gaps:
                        for v in range(g * slots, (g + 1) * slots):
                            abuf[p, v] = jnp.zeros(abuf.shape[2:], abuf.dtype)
                    return carry

                lax.fori_loop(0, rows, clear, 0)

    pltpu.make_async_copy(lbuf, lbuf, l_recv).wait()
    lanes = lbuf.shape[2]

    def match(p, carry):
        column_row = lbuf[p, 0:1, :]
        place = lbuf[p, 1:2, :]
        table = lbuf[(p // run * n_col + col) * n_depth, 8:, :]
        at = lax.broadcasted_iota(jnp.int32, (run, lanes), 0)
        wanted = jnp.sum(jnp.where(at == place, table, 0), axis=0, keepdims=True)
        hit = (keys_ref[1] == column_row) & (keys_ref[0] == wanted)
        number = lax.broadcasted_iota(jnp.int32, (blocks, lanes), 0)
        picks[pl.ds(p, 1), :] = jnp.min(
            jnp.where(hit, number, blocks), axis=0, keepdims=True
        )
        return carry

    lax.fori_loop(0, rows, match, 0)
    for q in range(run):
        picks[pl.ds(rows + q, 1), :] = lbuf[row * run + q, 1:2, :]
    to_scalars = pltpu.make_async_copy(picks, pick_s, s_sem)
    to_scalars.start()
    to_scalars.wait()

    def share_copy(target_row, d, slot):
        return pltpu.make_async_remote_copy(
            src_ref=cbuf.at[target_row, d],
            dst_ref=pbuf.at[slot],
            send_sem=c_send.at[target_row, d],
            recv_sem=c_recv.at[slot],
            device_id=(target_row, col, d),
            device_id_type=MESH,
        )

    def start_share(target_row, d, slot):
        own = (target_row == row) & (depth == d)

        @pl.when(jnp.logical_not(own))
        def _():
            share_copy(target_row, d, slot).start()

        @pl.when(own)
        def _():
            pltpu.make_async_copy(cbuf.at[target_row, d], pbuf.at[slot], c_recv.at[slot]).start()

    def settle_share(target_row, d):
        @pl.when(jnp.logical_not((target_row == row) & (depth == d)))
        def _():
            share_copy(target_row, d, 0).wait_send()

    is_paired = functools.reduce(jnp.logical_or, [my_rel == rel for rel in paired], False)

    def mate_copy(t, target_row):
        return pltpu.make_async_remote_copy(
            src_ref=cbuf.at[target_row, 1 - depth],
            dst_ref=mbuf.at[t % 2],
            send_sem=m_send.at[t % 2],
            recv_sem=m_recv.at[t % 2],
            device_id=(row, col, 1 - depth),
            device_id_type=MESH,
        )

    @pl.when(active)
    def _():
        b_copy.wait()
        bbuf[blocks] = jnp.zeros(bbuf.shape[1:], bbuf.dtype)

        def one_run(t, carry):
            target_row = flip(col, n_row - 1 - t, n_row)

            def one_row(q, inner):
                p = target_row * run + q
                for rel in rels:

                    @pl.when(my_rel == rel)
                    def _(rel=rel):
                        part = a_part(abuf.at[p], rel)
                        pltpu.make_async_copy(part, part, a_recv.at[p]).wait()

                for u in range(0, targets, 2):
                    total = None
                    for v in range(0, width, 2):
                        left = jnp.concatenate([abuf[p, v], abuf[p, v + 1]], axis=1)
                        right = jnp.concatenate(
                            [
                                jnp.concatenate(
                                    [
                                        bbuf[pick_s[p, (v + i) * targets + u]],
                                        bbuf[pick_s[p, (v + i) * targets + u + 1]],
                                    ],
                                    axis=1,
                                )
                                for i in range(2)
                            ],
                            axis=0,
                        )
                        term = jnp.dot(left, right, preferred_element_type=jnp.float32)
                        total = term if total is None else total + term
                    edge = abuf.shape[-1]
                    for i in range(2):
                        cbuf[target_row, (u + i) // share, q, (u + i) % share] = total[
                            :, i * edge : (i + 1) * edge
                        ].astype(cbuf.dtype)
                return inner

            lax.fori_loop(0, run, one_row, 0)
            for rel in lone:

                @pl.when(my_rel == rel)
                def _(rel=rel):
                    for d in range(n_depth):
                        start_share(target_row, d, sender(rel))

            if paired:

                @pl.when(is_paired)
                def _():
                    @pl.when(t >= 2)
                    def _():
                        pl.semaphore_wait(m_free, 1)

                    exchange = mate_copy(t, target_row)
                    exchange.start()
                    exchange.wait()

                    def merge(q, inner):
                        for u in range(share):
                            cbuf[target_row, depth, q, u] = (
                                cbuf[target_row, depth, q, u].astype(jnp.float32)
                                + mbuf[t % 2, q, u].astype(jnp.float32)
                            ).astype(cbuf.dtype)
                        return inner

                    lax.fori_loop(0, run, merge, 0)

                    @pl.when(t < n_row - 2)
                    def _():
                        pl.semaphore_signal(
                            m_free,
                            inc=1,
                            device_id=(row, col, 1 - depth),
                            device_id_type=MESH,
                        )

                for slot, first in enumerate(senders):
                    if first in paired:

                        @pl.when(my_rel // 2 * 2 == first)
                        def _(slot=slot):
                            start_share(target_row, depth, slot)

            return carry

        lax.fori_loop(0, n_row, one_run, 0)

    for slot in range(len(senders)):
        pltpu.make_async_copy(pbuf.at[slot], pbuf.at[slot], c_recv.at[slot]).wait()

    def finish(i, carry):
        q = jnp.int32(0)
        for j in range(run):
            q = jnp.where(pick_s[rows + j, 0] == i, j, q)
        for u in range(share):
            value = pbuf[0, q, u].astype(jnp.float32)
            for slot in range(1, len(senders)):
                value = value + pbuf[slot, q, u].astype(jnp.float32)
            kept = keep_ref[i * share + u] > 0
            out_ref[i, u] = jnp.where(kept, value, jnp.float32(0.0)).astype(out_ref.dtype)
        return carry

    lax.fori_loop(0, run, finish, 0)

    sent = lbuf.at[pl.ds(0, rows - 1)]
    pltpu.make_async_copy(sent, sent, l_send).wait()
    for mine, remote in sends:
        @pl.when(jnp.logical_not(mine))
        def _(remote=remote):
            remote.wait_send()

    def settle(target_row, carry):
        for rel in lone:

            @pl.when(my_rel == rel)
            def _():
                for d in range(n_depth):
                    settle_share(target_row, d)

        if paired:

            @pl.when(is_paired)
            def _():
                settle_share(target_row, depth)

        return carry

    lax.fori_loop(0, n_row, settle, 0)


BATCH = 4
BY_MAIN_FIRST, VIA_RELAY, DIRECT = 0, 1, 2
ORDER = (
    (
        0xb1fd85a9, 0x7e10a5bc, 0x9afe862c, 0x4827ce31, 0x2db194f7, 0x5168ae40, 0xb42f8c70, 0xd4032c59,
        0x3ca02b1e, 0xc7bfae45, 0xba286c3, 0xd59e3c16, 0x8263a749, 0x9cea405f, 0x1b0a3e26, 0x18c6afe4,
        0xf628410a, 0xf5e4d0c8, 0x7204aeb1, 0x6c8d49a7, 0x3b70d2f8, 0xe54c682d, 0x295140ab, 0xd24ec5f0,
        0x3aedc2b7, 0x5ac1629e, 0xbf8640ae, 0xc35f7a19, 0xa6c920df, 0x741068c2, 0x90fe4b52, 0x5f136b47,
    ),
    (
        0xc460723e, 0x863f249d, 0x43b7d501, 0xbdf59a60, 0x3c6ae85, 0x93fbd7c2, 0x16a3de59, 0x7e6b8af1,
        0x748d5f96, 0x12d39860, 0x7d95e14f, 0xf0a2b784, 0x51f0cedb, 0x12d83b67, 0xd7845fc9, 0xb027d953,
        0x5ec937bd, 0x396ab127, 0xfc36d589, 0xbf1e2035, 0x1e4c596a, 0x937b0fa1, 0xfc3d768e, 0x9a63b178,
        0x9085641f, 0xf84d30b7, 0x7d15392c, 0xed28406b, 0x531b748e, 0xad593bef, 0x68d1ca73, 0x2a8e9cd0,
    ),
)
ROUTES = (
    0x56a0, 0x55a0, 0x5526, 0x568a, 0x144a, 0xa559, 0x65a2, 0x4489,
    0x65a0, 0xa518, 0x590a, 0x5608, 0x1642, 0x258a, 0x6682, 0x6652,
    0x8599, 0x8299, 0xa258, 0x8194, 0x2095, 0xa065, 0x245a, 0xa59,
    0x6211, 0x8a59, 0x655a, 0xa114, 0xa295, 0x9855, 0xa55, 0xa95,
)
BY_MAIN = (
    0x80c0b03, 0x100d143, 0x7c98, 0x9000e04, 0x20700090, 0x193e0000, 0xc28b0080, 0xc0d03010,
)
RELAYED = (
    (7, 16, 5, 28, 30, 31, 29, 17, 23, 20, 21, 25, 24),
    (2, 30, 27, 19, 20, 21, 29, 31, 28),
    (9, 31, 18, 19, 16, 17, 15, 30, 26, 24, 25, 23, 29, 28, 20, 5, 27, 22),
    (12, 21, 4, 5, 25, 29, 15, 22, 26, 23, 30, 18),
    (19, 10, 26, 27, 6, 2, 16, 9, 5, 8, 1, 13),
    (22, 0, 12, 13, 14, 15, 1, 16, 5, 6, 7, 8, 2, 3, 11, 26, 4, 9),
    (29, 1, 4, 12, 10, 11, 2, 0, 3),
    (24, 15, 26, 3, 0, 1, 2, 8, 14, 10, 11, 6, 7),
)
MAIN_ROWS = (
    (0, 1, 14, 3, 11, 2, 10, 27, 8, 22, 19, 9, 15, 26, 18, 7, 6, 30, 12, 13, 23, 20, 21, 25, 24, 29, 4, 31, 5, 28, 16, 17),
    (10, 11, 2, 1, 3, 13, 0, 8, 9, 14, 31, 6, 7, 16, 17, 24, 12, 19, 21, 4, 20, 25, 29, 28, 15, 22, 23, 30, 18, 5, 26, 27),
    (20, 21, 18, 28, 29, 30, 31, 23, 22, 17, 0, 25, 24, 14, 15, 12, 7, 19, 27, 10, 11, 2, 6, 3, 9, 16, 8, 1, 13, 5, 4, 26),
    (30, 31, 17, 28, 29, 20, 21, 4, 9, 22, 23, 12, 5, 16, 13, 24, 25, 1, 19, 18, 10, 8, 6, 11, 7, 2, 0, 3, 27, 26, 14, 15),
)
SIDE_ROWS = (
    (6, 7, 14, 15, 16, 5, 28, 2, 30, 31, 22, 29, 17, 23, 26, 20, 21, 12, 13, 4, 25, 24, 0, 1, 11, 10, 8, 3, 9, 19, 18, 27),
    (3, 2, 11, 30, 10, 23, 26, 18, 27, 7, 19, 20, 21, 16, 29, 4, 17, 22, 31, 0, 1, 28, 14, 8, 13, 9, 15, 12, 6, 25, 24, 5),
    (8, 9, 31, 18, 19, 0, 1, 16, 17, 22, 15, 30, 26, 24, 25, 6, 23, 5, 29, 2, 27, 10, 11, 3, 13, 14, 28, 7, 20, 12, 21, 4),
    (13, 12, 21, 14, 20, 4, 5, 28, 25, 29, 31, 15, 8, 19, 22, 16, 26, 23, 1, 7, 30, 6, 17, 18, 3, 10, 11, 2, 0, 9, 24, 27),
    (18, 19, 10, 11, 17, 26, 27, 3, 6, 2, 0, 16, 23, 12, 9, 15, 5, 8, 30, 24, 1, 25, 14, 13, 28, 20, 21, 29, 31, 22, 7, 4),
    (23, 22, 0, 12, 13, 30, 31, 14, 15, 9, 1, 16, 5, 6, 7, 25, 8, 26, 2, 29, 4, 20, 21, 18, 28, 17, 3, 24, 11, 19, 10, 27),
    (28, 29, 20, 1, 21, 5, 8, 13, 4, 24, 12, 10, 11, 15, 2, 27, 14, 9, 0, 30, 31, 3, 17, 22, 18, 23, 16, 19, 25, 6, 7, 26),
    (25, 24, 16, 17, 15, 26, 3, 29, 0, 1, 9, 2, 8, 14, 5, 10, 11, 18, 19, 27, 6, 7, 30, 31, 20, 21, 22, 28, 23, 12, 13, 4),
)


def pick_word(words, index):
    value = jnp.int32(0)
    for i, word in enumerate(words):
        word = jnp.int32(word - (1 << 32) if word >> 31 else word)
        value = jnp.where(index == i, word, value)
    return value


def field(word, index, bits):
    return lax.shift_right_logical(word, index * bits) & ((1 << bits) - 1)


def torus_kernel(
    total,
    pack_ref, keys_ref, a_ref, b_ref, out_ref,
    lbuf, picks, pick_s, abuf, bbuf, cbuf, mbuf, pbuf,
    l_send, l_recv, s_sem, b_sem, a_send, a_recv, f_send,
    m_send, m_recv, c_send, c_recv,
):
    n_row, n_col, n_depth = 4, 4, 2
    row, col, depth = (lax.axis_index(name) for name in ("row", "col", "depth"))
    run = n_col * n_depth
    rows = n_row * run
    me = (row * n_col + col) * n_depth + depth
    my_stripe = row * n_depth + depth
    blocks = b_ref.shape[0]
    share = pbuf.shape[2]
    targets = share * n_depth
    width = abuf.shape[1]
    half = width // 2
    edge = abuf.shape[-1]
    outer = side_col(row, depth)
    is_main = col == row
    is_side = col == outer
    is_relay = col == side_col(row, 1 - depth)
    active = is_main | is_side
    my_edge = depth * half

    def list_copy(offset):
        dest = lax.rem(me + offset, rows)
        dest_row, dest_col, dest_depth = dest // run, dest // n_depth % n_col, dest % n_depth
        return pltpu.make_async_remote_copy(
            src_ref=pack_ref.at[dest_row * n_depth + dest_depth],
            dst_ref=lbuf.at[me],
            send_sem=l_send,
            recv_sem=l_recv,
            device_id=(dest_row, dest_col, dest_depth),
            device_id_type=MESH,
        )

    pltpu.make_async_copy(pack_ref.at[my_stripe], lbuf.at[me], l_recv).start()

    def send_list(offset, carry):
        list_copy(offset).start()
        return carry

    lax.fori_loop(1, rows, send_list, 0)

    b_copy = pltpu.make_async_copy(b_ref, bbuf.at[pl.ds(0, blocks)], b_sem)

    @pl.when(active)
    def _():
        b_copy.start()

    sends = []

    def send_part(wanted, src, low, place):
        mine = (row == place[0]) & (col == place[1]) & (depth == place[2])
        dst = abuf.at[me, pl.ds(low, half)]
        remote = pltpu.make_async_remote_copy(
            src_ref=src,
            dst_ref=dst,
            send_sem=a_send.at[len(sends)],
            recv_sem=a_recv.at[me],
            device_id=place,
            device_id_type=MESH,
        )
        local = pltpu.make_async_copy(src, dst, a_recv.at[me])
        away = wanted & jnp.logical_not(mine)
        sends.append((away, remote))

        @pl.when(wanted & mine)
        def _():
            local.start()

        @pl.when(away)
        def _():
            remote.start()

    my_order = [pick_word(words, me) for words in ORDER]
    my_routes = pick_word(ROUTES, me)
    for t in range(2 * n_col * n_depth):
        entry = field(my_order[t // 8], t % 8, 4)
        s, is_mid = entry // 2, entry % 2 == 1
        c, d = s // n_depth, s % n_depth
        route = field(my_routes, s, 2)
        side = side_col(c, d)
        low = jnp.where(is_mid, half - d * half, d * half)
        src = a_ref.at[pl.ds(s * width + low, half)]
        via = (route == VIA_RELAY) & jnp.logical_not(is_mid)
        place = (c, jnp.where(via, side, c), jnp.where(via, 1 - d, d))
        send_part(me >= 0, src, low, place)
        twice = (route == DIRECT) & jnp.logical_not(is_mid)
        send_part(twice, src, low, (c, side, d))

    far_edge = (1 - depth) * half

    def relay_copy(p, dest_col):
        part = abuf.at[p, pl.ds(far_edge, half)]
        return pltpu.make_async_remote_copy(
            src_ref=part,
            dst_ref=part,
            send_sem=f_send.at[p],
            recv_sem=a_recv.at[p],
            device_id=(row, dest_col, 1 - depth),
            device_id_type=MESH,
        )

    def wait_blocks(p, count):
        part = abuf.at[p, pl.ds(0, count)]
        pltpu.make_async_copy(part, part, a_recv.at[p]).wait()

    other_stripe = row * n_depth + 1 - depth
    relayed_rows = pick_word([len(r) for r in RELAYED], other_stripe)
    relay_words = [
        pick_word([pack_bytes(r)[w] for r in RELAYED], other_stripe) for w in range(rows // 4)
    ]

    def table_row(words, i):
        word = words[0]
        for w in range(1, len(words)):
            word = jnp.where(i // 4 == w, words[w], word)
        return field(word, i % 4, 8)

    @pl.when(is_relay)
    def _():
        def relay(i, carry):
            p = table_row(relay_words, i)
            wait_blocks(p, half)
            relay_copy(p, row).start()
            relay_copy(p, col).start()
            return carry

        lax.fori_loop(0, relayed_rows, relay, 0)

    pltpu.make_async_copy(lbuf, lbuf, l_recv).wait()
    lanes = lbuf.shape[2]

    def match(p, carry):
        column_row = lbuf[p, 0:1, :]
        place = lbuf[p, 1:2, :]
        table = lbuf[(p // run * n_col + col) * n_depth, 8:, :]
        at = lax.broadcasted_iota(jnp.int32, (run, lanes), 0)
        wanted = jnp.sum(jnp.where(at == place, table, 0), axis=0, keepdims=True)
        hit = keys_ref[...] == column_row * total + wanted
        number = lax.broadcasted_iota(jnp.int32, (blocks, lanes), 0)
        picks[pl.ds(p, 1), :] = jnp.min(
            jnp.where(hit, number, blocks), axis=0, keepdims=True
        )
        return carry

    lax.fori_loop(0, rows, match, 0)
    for q in range(run):
        picks[pl.ds(rows + q, 1), :] = lbuf[row * run + q, 1:2, :]
    to_scalars = pltpu.make_async_copy(picks, pick_s, s_sem)
    to_scalars.start()
    to_scalars.wait()

    main_words = [pick_word([pack_bytes(r)[w] for r in MAIN_ROWS], row) for w in range(run)]
    side_words = [pick_word([pack_bytes(r)[w] for r in SIDE_ROWS], my_stripe) for w in range(run)]
    by_main = pick_word(BY_MAIN, my_stripe)

    def forward_copy(p, dest_col):
        part = abuf.at[p, pl.ds(my_edge, half)]
        return pltpu.make_async_remote_copy(
            src_ref=part,
            dst_ref=part,
            send_sem=f_send.at[p],
            recv_sem=a_recv.at[p],
            device_id=(row, dest_col, depth),
            device_id_type=MESH,
        )

    def batch_rows(words, b):
        return [table_row(words, b * BATCH + i) for i in range(BATCH)]

    def multiply(p, b, at, base, count):
        left = jnp.concatenate([abuf[p, base + v] for v in range(count)], axis=1)
        for u in range(0, targets, 2):
            right = jnp.concatenate(
                [
                    jnp.concatenate(
                        [
                            bbuf[pick_s[p, (base + v) * targets + u]],
                            bbuf[pick_s[p, (base + v) * targets + u + 1]],
                        ],
                        axis=1,
                    )
                    for v in range(count)
                ],
                axis=0,
            )
            total = jnp.dot(left, right, preferred_element_type=jnp.float32)
            for i in range(2):
                cbuf[(u + i) // share, b, at, (u + i) % share] = total[
                    :, i * edge : (i + 1) * edge
                ].astype(cbuf.dtype)

    def start_share(p, b, at, d, slot):
        target, q = p // run, p % run
        own = (row == target) & (depth == d)
        src = cbuf.at[d, b, at]
        dst = pbuf.at[slot, q]

        @pl.when(jnp.logical_not(own))
        def _():
            pltpu.make_async_remote_copy(
                src_ref=src,
                dst_ref=dst,
                send_sem=c_send,
                recv_sem=c_recv.at[slot],
                device_id=(target, col, d),
                device_id_type=MESH,
            ).start()

        @pl.when(own)
        def _():
            pltpu.make_async_copy(src, dst, c_recv.at[slot]).start()

    def mate_copy(b):
        return pltpu.make_async_remote_copy(
            src_ref=cbuf.at[1 - depth, b],
            dst_ref=mbuf.at[b],
            send_sem=m_send,
            recv_sem=m_recv.at[b],
            device_id=(row, col, 1 - depth),
            device_id_type=MESH,
        )

    @pl.when(active)
    def _():
        b_copy.wait()
        bbuf[blocks] = jnp.zeros(bbuf.shape[1:], bbuf.dtype)

    @pl.when(is_main)
    def _():
        def one_batch(b, carry):
            @pl.when(b < rows // BATCH)
            def _():
                members = batch_rows(main_words, b)
                for p in members:

                    @pl.when(field(by_main, p, 1) == 1)
                    def _(p=p):
                        wait_blocks(p, width)
                        forward_copy(p, outer).start()

                for p in members:

                    @pl.when(field(by_main, p, 1) == 0)
                    def _(p=p):
                        wait_blocks(p, width)

                def one_row(i, inner):
                    multiply(table_row(main_words, b * BATCH + i), b, i, 0, width)
                    return inner

                lax.fori_loop(0, BATCH, one_row, 0)
                mate_copy(b).start()

            @pl.when(b > 0)
            def _():
                last = b - 1
                pltpu.make_async_copy(mbuf.at[last], mbuf.at[last], m_recv.at[last]).wait()

                def merge(i, inner):
                    for u in range(share):
                        cbuf[depth, last, i, u] = (
                            cbuf[depth, last, i, u].astype(jnp.float32)
                            + mbuf[last, i, u].astype(jnp.float32)
                        ).astype(cbuf.dtype)
                    return inner

                lax.fori_loop(0, BATCH, merge, 0)
                for i, p in enumerate(batch_rows(main_words, last)):
                    start_share(p, last, i, depth, 0)

            return carry

        lax.fori_loop(0, rows // BATCH + 1, one_batch, 0)

    @pl.when(is_side)
    def _():
        def one_batch(b, carry):
            members = batch_rows(side_words, b)
            for p in members:
                wait_blocks(p, half)

            def one_row(i, inner):
                multiply(table_row(side_words, b * BATCH + i), b, i, my_edge, half)
                return inner

            lax.fori_loop(0, BATCH, one_row, 0)
            for i, p in enumerate(members):
                for d in range(n_depth):
                    start_share(p, b, i, d, 1 + depth)
            return carry

        lax.fori_loop(0, rows // BATCH, one_batch, 0)

    for slot in range(pbuf.shape[0]):
        pltpu.make_async_copy(pbuf.at[slot], pbuf.at[slot], c_recv.at[slot]).wait()

    def finish(i, carry):
        q = jnp.int32(0)
        for j in range(run):
            q = jnp.where(pick_s[rows + j, 0] == i, j, q)
        for u in range(share):
            value = pbuf[0, q, u].astype(jnp.float32)
            for slot in range(1, pbuf.shape[0]):
                value = value + pbuf[slot, q, u].astype(jnp.float32)
            out_ref[i, u] = value.astype(out_ref.dtype)
        return carry

    lax.fori_loop(0, run, finish, 0)

    sent = lbuf.at[pl.ds(0, rows - 1)]
    pltpu.make_async_copy(sent, sent, l_send).wait()
    for away, remote in sends:

        @pl.when(away)
        def _(remote=remote):
            remote.wait_send()

    @pl.when(is_relay)
    def _():
        def settle(i, carry):
            part = abuf.at[0]
            pltpu.make_async_copy(part, part, f_send.at[table_row(relay_words, i)]).wait()
            return carry

        lax.fori_loop(0, relayed_rows, settle, 0)

    @pl.when(is_main)
    def _():
        def settle(p, carry):
            @pl.when(field(by_main, p, 1) == 1)
            def _():
                forward_copy(p, outer).wait_send()

            return carry

        lax.fori_loop(0, rows, settle, 0)
        pltpu.make_async_copy(mbuf, mbuf, m_send).wait()
        part = abuf.at[pl.ds(0, (rows - run) * share // width)]
        pltpu.make_async_copy(part, part, c_send).wait()

    @pl.when(is_side)
    def _():
        part = abuf.at[pl.ds(0, (2 * rows - run) * share // width)]
        pltpu.make_async_copy(part, part, c_send).wait()


def side_col(column, depth):
    return lax.rem(column + 2 * depth + 3, 4)


def pack_bytes(members):
    padded = list(members) + [0] * (32 - len(members))
    return [sum(padded[4 * w + i] << (8 * i) for i in range(4)) for w in range(8)]


def on_device(
    a_blocks, a_columns, a_live, atom_rows, b_blocks, b_columns, b_live, c_columns, c_live
):
    n_row, n_col, n_depth = (lax.axis_size(name) for name in ("row", "col", "depth"))
    row, depth = (lax.axis_index(name) for name in ("row", "depth"))
    _, group_count, slots = a_columns.shape
    edge = a_blocks.shape[-1]
    stripe, _, list_width = b_columns.shape
    run, _, targets = c_columns.shape
    stripes = n_row * n_depth
    total = stripe * stripes
    share = targets // n_depth
    width = group_count * slots // stripes
    row_count = n_row * run
    kinds = stripe_kinds(total, stripe, total // n_col)
    senders = {rel // 2 * 2 if rel ^ 1 in kinds and n_depth == 2 else rel for rel in kinds}
    block_count = stripe * list_width
    lanes = -(-width * targets // 128) * 128
    spare = lanes - width * targets

    firsts = jnp.arange(stripes, dtype=jnp.int32)[:, None] * stripe
    a_keys = jnp.where(a_live > 0, a_columns, -total).reshape(stripes, width) - firsts
    a_keys = jnp.repeat(a_keys, targets, axis=1)
    a_keys = jnp.pad(a_keys, ((0, 0), (0, spare)), constant_values=-1)[:, None]
    place = jnp.broadcast_to((atom_rows - row * run).reshape(1, 1, 1), (stripes, 1, lanes))
    table = jnp.tile(c_columns[:, 0, :], (1, width))
    table = jnp.pad(table, ((0, 0), (0, spare)), constant_values=-2)
    pack = jnp.concatenate(
        [
            a_keys,
            place,
            jnp.zeros((stripes, 6, lanes), jnp.int32),
            jnp.broadcast_to(table[None], (stripes, run, lanes)),
        ],
        axis=1,
    )
    b_keys = jnp.where(b_live > 0, b_columns, -1).reshape(-1)
    b_rows = jnp.arange(block_count, dtype=jnp.int32) // list_width
    blocks = (a_blocks.reshape(-1, edge, edge), b_blocks.reshape(-1, edge, edge))
    lists = [
        pltpu.VMEM((row_count, 8 + run, lanes), jnp.int32),
        pltpu.VMEM((row_count + run, lanes), jnp.int32),
        pltpu.SMEM((row_count + run, lanes), jnp.int32),
        pltpu.VMEM((row_count, width, edge, edge), jnp.bfloat16),
        pltpu.VMEM((block_count + 1, edge, edge), jnp.bfloat16),
    ]
    relayed = (n_row, n_col, n_depth) == (4, 4, 2) and sorted(kinds) == [0, 1, 2, 7]
    if relayed:
        body = functools.partial(torus_kernel, total)
        codes = jnp.where(b_keys >= 0, b_rows * total + b_keys, -1)
        keys = jnp.broadcast_to(codes[:, None], (block_count, lanes))
        lead, places = (pack, keys), []
        scratch = lists + [
            pltpu.VMEM((n_depth, row_count // BATCH, BATCH, share, edge, edge), jnp.bfloat16),
            pltpu.VMEM((row_count // BATCH, BATCH, share, edge, edge), jnp.bfloat16),
            pltpu.VMEM((3, run, share, edge, edge), jnp.bfloat16),
            pltpu.SemaphoreType.DMA,
            pltpu.SemaphoreType.DMA,
            pltpu.SemaphoreType.DMA,
            pltpu.SemaphoreType.DMA,
            pltpu.SemaphoreType.DMA((4 * n_col * n_depth,)),
            pltpu.SemaphoreType.DMA((row_count,)),
            pltpu.SemaphoreType.DMA((row_count,)),
            pltpu.SemaphoreType.DMA,
            pltpu.SemaphoreType.DMA((row_count // BATCH,)),
            pltpu.SemaphoreType.DMA,
            pltpu.SemaphoreType.DMA((3,)),
        ]
    else:
        body = functools.partial(kernel, n_row, n_col, n_depth, kinds, slots)
        keys = jnp.stack([b_keys, b_rows])[:, :, None]
        keys = jnp.broadcast_to(keys, (2, block_count, lanes))
        keep = lax.dynamic_slice_in_dim(c_live[:, 0, :], depth * share, share, 1).reshape(-1)
        lead, places = (pack, keys, keep), [pl.BlockSpec(memory_space=pltpu.SMEM)]
        scratch = lists + [
            pltpu.VMEM((n_row, n_depth, run, share, edge, edge), jnp.bfloat16),
            pltpu.VMEM((2, run, share, edge, edge), jnp.bfloat16),
            pltpu.VMEM((len(senders), run, share, edge, edge), jnp.bfloat16),
            pltpu.SemaphoreType.DMA,
            pltpu.SemaphoreType.DMA,
            pltpu.SemaphoreType.DMA,
            pltpu.SemaphoreType.DMA,
            pltpu.SemaphoreType.DMA((n_col * len(kinds),)),
            pltpu.SemaphoreType.DMA((row_count,)),
            pltpu.SemaphoreType.DMA((2,)),
            pltpu.SemaphoreType.DMA((2,)),
            pltpu.SemaphoreType.REGULAR,
            pltpu.SemaphoreType.DMA((n_row, n_depth)),
            pltpu.SemaphoreType.DMA((len(senders),)),
        ]
    result = pl.pallas_call(
        body,
        out_shape=jax.ShapeDtypeStruct((run, share, edge, edge), jnp.bfloat16),
        in_specs=[
            pl.BlockSpec(memory_space=pltpu.VMEM),
            pl.BlockSpec(memory_space=pltpu.VMEM),
            *places,
            pl.BlockSpec(memory_space=pl.ANY),
            pl.BlockSpec(memory_space=pl.ANY),
        ],
        out_specs=pl.BlockSpec(memory_space=pltpu.VMEM),
        scratch_shapes=scratch,
        compiler_params=pltpu.CompilerParams(
            has_side_effects=True, vmem_limit_bytes=60 * 1024 * 1024
        ),
    )(*lead, *blocks)
    if relayed:
        wanted = lax.dynamic_slice_in_dim(c_live, depth * share, share, 2) > 0
        return jnp.where(wanted[..., None, None], result[:, None], jnp.bfloat16(0.0))
    return result[:, None]


def solution(mesh):
    placed = (
        P(("row", "col", "depth"), None, None, None, None),
        P(("row", "col", "depth"), None, None),
        P(("row", "col", "depth"), None, None),
        P(("row", "col", "depth")),
        P(("row", "depth"), "col", None, None, None),
        P(("row", "depth"), "col", None),
        P(("row", "depth"), "col", None),
        P("row", "col", None),
        P("row", "col", None),
    )
    return jax.shard_map(
        on_device,
        mesh=mesh,
        in_specs=placed,
        out_specs=P("row", "col", "depth", None, None),
        check_vma=False,
    )
```
